256 devices in a mesh: dp: 8 (over z), seq: 32 (over x, y, core).
Axes of the slice: x: 4, y: 4, z: 8, core: 2. Of those that a mesh axis runs over, the one named last changes fastest.
Arguments:
- values_in: bfloat16 [8, 4096, 2048], P('dp', 'seq'), may hold values from -6 to 6
- input_proj: bfloat16 [8, 4096, 128], P('dp', 'seq'), may hold values from -0.5 to 0.5
- output_proj: bfloat16 [8, 4096, 128], P('dp', 'seq'), may hold values from -0.09375 to 0.09375
- log_decay: float32 [8, 32, 4096], P('dp', None, 'seq'), may hold values from -1 to 0, as said below
- doc_lengths: int32 [8, 8], P('dp'), may hold values from 1 to 2048, 4096 in all within a row
- skip_gain: float32 [32], replicated, may hold values from 0.5 to 1.5
- out_cotangent: bfloat16 [8, 4096, 2048], P('dp', 'seq'), may hold values from -6 to 6
Outputs:
- mixed_out: bfloat16 [8, 4096, 2048], P('dp', 'seq')
- values_grad: bfloat16 [8, 4096, 2048], P('dp', 'seq')
- input_grad: float32 [8, 4096, 128], P('dp', 'seq')
- output_grad: float32 [8, 4096, 128], P('dp', 'seq')
- decay_grad: float32 [8, 32, 4096], P('dp', None, 'seq')
- skip_grad: float32 [32], replicated
The draws below stay inside these ranges and needn't reach their ends.
Inputs may be any that keep to these rules, and one draw needn't show every extreme that they name: `doc_lengths`: one row lists the documents of one sequence in order and sums to 4096. `log_decay`: negative log decay of each head at each token.
All inputs are finite; a program needn't handle non-finite values.
Results may differ from the reference program's by a relative error of at most 0.0056.
Values sent between devices are 32-bit elements; how exact they have to be, the bound alone decides.
No kernel may reach another device: no remote copies, remote signals or barrier semaphores. Data moves between devices by JAX's collectives and lax.ppermute only.
A program may use at most 128 MiB of HBM per device.

```python
import math
import jax
import jax.numpy as jnp
import numpy as np
from jax import lax

HEADS = 32
STATE = 128
TOK_DEV = 128
DOCS = 8
PACKED_SEQUENCES = 8
SEQUENCE_TOKENS = 4096
INNER = 2048


def draw_log_decay(key, part):
    random_subkeys = jax.random.split(key, 7)
    slow_share = 0.5
    complete_shape = (PACKED_SEQUENCES, HEADS, SEQUENCE_TOKENS)
    head_shape = (PACKED_SEQUENCES, HEADS, 1)
    slow_flag = jax.random.uniform(random_subkeys[0], head_shape) < slow_share
    slow_rate = jnp.exp(jax.random.uniform(random_subkeys[1], head_shape, minval=math.log(0.05), maxval=math.log(0.5))) / SEQUENCE_TOKENS
    fast_rate = jnp.exp(jax.random.uniform(random_subkeys[2], head_shape, minval=math.log(1.0 / 50.0), maxval=math.log(1.0 / 30.0)))
    baseline_rate = jnp.where(slow_flag, slow_rate, fast_rate)
    partition_factor = jnp.exp(jax.random.uniform(random_subkeys[3], (PACKED_SEQUENCES, 1, SEQUENCE_TOKENS // TOK_DEV), minval=math.log(0.7), maxval=math.log(1.4)))
    partition_factor = jnp.repeat(partition_factor, TOK_DEV, axis=2)
    token_multiplier = jnp.exp(jax.random.uniform(random_subkeys[4], complete_shape, minval=math.log(0.6), maxval=math.log(1.6)))
    spike_positions = jax.random.randint(random_subkeys[5], (PACKED_SEQUENCES, 1, 2), 0, SEQUENCE_TOKENS)
    token_position_index = jnp.arange(SEQUENCE_TOKENS, dtype=jnp.int32)
    spike_mask = jnp.any(token_position_index[None, None, :, None] == spike_positions[:, :, None, :], axis=3)
    spike_length = jax.random.uniform(random_subkeys[6], complete_shape, minval=0.22, maxval=0.69)
    logarithm_values = -(baseline_rate * partition_factor * token_multiplier) - jnp.where(spike_mask, spike_length, 0.0)
    return logarithm_values.astype(jnp.float32)


def block_scale(key, dims, shards, low, top_value):
    factor_of = 1.0
    for dim, shards_of in shards:
        draws = jax.random.uniform(jax.random.fold_in(jax.random.fold_in(key, 6), dim), (shards_of,), jnp.float32, low / len(shards), top_value / len(shards))
        factor_of = factor_of * jnp.repeat(jnp.exp(draws), dims[dim] // shards_of).reshape((-1,) + (1,) * (len(dims) - 1 - dim))
    return factor_of


def split_up(number_of, total, most, slope):
    portions = [(1 << 20) // math.isqrt(standing ** slope) + 1 for standing in range(2, number_of + 1)]
    rest, counts = total - most - (number_of - 1), [1] * (number_of - 1)
    while rest > 0:
        movable = [i for i in range(number_of - 1) if counts[i] < most]
        whole, left = sum([portions[i] for i in movable]), rest
        for i in movable:
            extra = min(most - counts[i], max(1, left * portions[i] // whole), rest)
            counts[i] = counts[i] + extra
            rest = rest - extra
    return np.array([most] + counts)


def ragged_sizes(key, count, total, limit, slope):
    if count == 2:
        one = jax.random.randint(key, (), max(1, total - limit), min(limit, total - 1) + 1)
        return jnp.stack([one, total - one])
    sizes = jnp.asarray(split_up(count, total, limit, slope), jnp.int32)
    pairs = (count - 1) // 2
    source_of, sink = sizes[1:1 + 2 * pairs:2], sizes[2:2 + 2 * pairs:2]
    slack = jnp.minimum(source_of - 1, limit - sink)
    shifted = jax.random.randint(jax.random.fold_in(key, 1), (pairs,), 0, 1 << 20) % (slack + 1)
    sizes = sizes.at[1:1 + 2 * pairs:2].set(source_of - shifted).at[2:2 + 2 * pairs:2].set(sink + shifted)
    return sizes[jax.random.permutation(jax.random.fold_in(key, 2), count)]


def centred(rng, dims, spread, limit, cuts=(), held_as=jnp.bfloat16):
    values = jax.random.normal(rng, dims, jnp.float32) * spread
    if len(cuts) > 0:
        values = block_scale(rng, dims, cuts, -0.22, 0.18) * values
    return jnp.clip(values, min=-limit, max=limit).astype(held_as)


def setup_inputs(seed: int = 0) -> dict:
    streams_of = jax.random.split(jax.random.key(seed), 8)
    return {
        "values_in": centred(streams_of[0], (PACKED_SEQUENCES, SEQUENCE_TOKENS, INNER), 1.0, 6.0, ((0, 8), (1, 32))),
        "input_proj": centred(streams_of[1], (PACKED_SEQUENCES, SEQUENCE_TOKENS, STATE), STATE ** -0.5, 0.5, ((0, 8), (1, 32))),
        "output_proj": centred(streams_of[2], (PACKED_SEQUENCES, SEQUENCE_TOKENS, STATE), SEQUENCE_TOKENS ** -0.5, 0.09375, ((0, 8), (1, 32))),
        "log_decay": draw_log_decay(jax.random.fold_in(streams_of[7], 71), 0),
        "doc_lengths": jax.vmap(lambda own: ragged_sizes(own, DOCS, SEQUENCE_TOKENS, SEQUENCE_TOKENS // 2, 2))(jax.random.split(streams_of[4], PACKED_SEQUENCES)).reshape((PACKED_SEQUENCES, DOCS)).astype(jnp.int32),
        "skip_gain": jnp.clip(jax.random.uniform(streams_of[5], (HEADS,), jnp.float32, 0.5, 1.5), 0.5, 1.5),
        "out_cotangent": centred(streams_of[6], (PACKED_SEQUENCES, SEQUENCE_TOKENS, INNER), 1.0, 6.0, ((0, 8), (1, 32))),
    }


def product(form, left_side, right_side):
    return jnp.einsum(form, left_side.astype(jnp.float32), right_side.astype(jnp.float32), precision=lax.Precision.HIGHEST)

def block_stats(log_rows, resets):
    log_cum = jnp.cumsum(log_rows, axis=1)
    seg_count = jnp.cumsum(resets)
    log_end = log_cum[:, -1:]
    count_end = seg_count[-1]
    carry_gain = jnp.exp(log_end[:, 0]) * (count_end == 0).astype(jnp.float32)
    weight_end = jnp.exp(log_end - log_cum) * (seg_count == count_end).astype(jnp.float32)[None, :]
    weight_start = jnp.exp(log_cum) * (seg_count == 0).astype(jnp.float32)[None, :]
    return (log_cum, seg_count, carry_gain, weight_end, weight_start)

def head_scale(values, factors):
    row_count, inner_width = values.shape
    head_count = factors.shape[0]
    shaped = values.reshape(row_count, head_count, inner_width // head_count)
    return (shaped * factors.T[:, :, None]).reshape(row_count, inner_width)

def head_dot(left_side, right_side, head_count):
    row_count = left_side.shape[0]
    joined = left_side.astype(jnp.float32) * right_side.astype(jnp.float32)
    return lax.optimization_barrier(jnp.sum(joined.reshape(row_count, head_count, -1), axis=2)).T

def prepare_block(values, input_rows, output_rows, grads_in, log_rows, resets):
    log_cum, seg_count, carry_gain, weight_end, weight_start = block_stats(log_rows, resets)
    weighted_values = head_scale(values, weight_end).astype(jnp.bfloat16)
    weighted_grads = head_scale(grads_in, weight_start).astype(jnp.bfloat16)
    local_state = product('li,ln->in', weighted_values, input_rows)
    local_adjoint = product('li,ln->in', weighted_grads, output_rows)
    return (local_state, local_adjoint, carry_gain, weighted_values, weighted_grads)

def finish_block(values, input_rows, output_rows, grads_in, log_rows, resets, skip_gain, state_in, adjoint_in):
    log_cum, seg_count, carry_gain, weight_end, weight_start = block_stats(log_rows, resets)
    weighted_values = head_scale(values, weight_end).astype(jnp.bfloat16)
    weighted_grads = head_scale(grads_in, weight_start).astype(jnp.bfloat16)
    head_count = log_cum.shape[0]
    row_count, inner_width = values.shape
    head_dim = inner_width // head_count
    state_half = state_in.astype(jnp.bfloat16)
    adjoint_half = adjoint_in.astype(jnp.bfloat16)
    state_read = product('ln,in->li', output_rows, state_half)
    adjoint_read = product('ln,in->li', input_rows, adjoint_half)
    scores = product('tn,sn->ts', output_rows, input_rows)
    position = jnp.arange(row_count, dtype=jnp.int32)
    causal = (position[None, :] <= position[:, None]) & (seg_count[None, :] == seg_count[:, None])
    group_size = min(4, head_count)
    outs_within = []
    outs_back = []
    grad_parts = []
    grad_scores = jnp.zeros((row_count, row_count), jnp.float32)
    for block_index in range(head_count // group_size):
        first_head = block_index * group_size
        low_col = first_head * head_dim
        high_col = (first_head + group_size) * head_dim
        value_group = values[:, low_col:high_col].reshape(row_count, group_size, head_dim)
        grad_group = grads_in[:, low_col:high_col].reshape(row_count, group_size, head_dim)
        log_group = log_cum[first_head:first_head + group_size]
        log_gap = log_group[:, :, None] - log_group[:, None, :]
        decay_mat = jnp.exp(jnp.where(causal[None], log_gap, -jnp.inf))
        weighted = scores[None] * decay_mat
        mix_half = weighted.astype(jnp.bfloat16)
        outs_within.append(product('gts,sgp->tgp', mix_half, value_group).reshape(row_count, -1))
        outs_back.append(product('gts,tgp->sgp', mix_half, grad_group).reshape(row_count, -1))
        grad_mix = product('tgp,sgp->gts', grad_group, value_group)
        sensitivity = grad_mix * weighted
        grad_parts.append(lax.optimization_barrier(jnp.sum(sensitivity, axis=2)) - lax.optimization_barrier(jnp.sum(sensitivity, axis=1)))
        grad_scores = grad_scores + lax.optimization_barrier(jnp.sum(grad_mix * decay_mat, axis=0))
    within_out = jnp.concatenate(outs_within, axis=1)
    back_part = jnp.concatenate(outs_back, axis=1)
    grad_cum = jnp.concatenate(grad_parts, axis=0)
    skip_rows = jnp.repeat(skip_gain, head_dim)[None, :]
    mixed = (within_out + head_scale(state_read, weight_start) + skip_rows * values).astype(jnp.bfloat16)
    values_grad = (back_part + head_scale(adjoint_read, weight_end) + skip_rows * grads_in).astype(jnp.bfloat16)
    grad_start = head_dot(grads_in, state_read, head_count)
    grad_end = head_dot(values, adjoint_read, head_count)
    grad_gain = lax.optimization_barrier(jnp.sum((state_in * adjoint_in).reshape(head_count, -1), axis=1))
    end_total = lax.optimization_barrier(jnp.sum(weight_end * grad_end, axis=1)) + carry_gain * grad_gain
    grad_cum = grad_cum + weight_start * grad_start - weight_end * grad_end
    grad_cum = grad_cum.at[:, -1].add(end_total)
    decay_raw = jnp.flip(jnp.cumsum(jnp.flip(grad_cum, 1), axis=1), 1) * (1 - resets).astype(jnp.float32)[None, :]
    grad_half = grad_scores.astype(jnp.bfloat16)
    input_raw = product('ts,tn->sn', grad_half, output_rows) + product('li,in->ln', weighted_values, adjoint_half)
    output_raw = product('ts,sn->tn', grad_half, input_rows) + product('li,in->ln', weighted_grads, state_half)
    skip_part = lax.optimization_barrier(jnp.sum(head_dot(grads_in, values, head_count), axis=1))
    return (mixed, values_grad, input_raw, output_raw, decay_raw, skip_part)

def reference(values_in, input_proj, output_proj, log_decay, doc_lengths, skip_gain, out_cotangent):
    seq_count, token_count, inner_width = values_in.shape
    head_count = log_decay.shape[1]
    state_width = input_proj.shape[2]
    head_dim = inner_width // head_count
    blocks = token_count // TOK_DEV
    flat_count = seq_count * blocks
    position = jnp.arange(token_count, dtype=jnp.int32)
    starts = jnp.cumsum(doc_lengths, axis=1).astype(jnp.int32) - doc_lengths
    resets = jnp.any(position[None, :, None] == starts[:, None, :], axis=2).astype(jnp.int32)
    values_blocks = values_in.reshape(flat_count, TOK_DEV, inner_width)
    grads_blocks = out_cotangent.reshape(flat_count, TOK_DEV, inner_width)
    input_blocks = input_proj.reshape(flat_count, TOK_DEV, state_width)
    output_blocks = output_proj.reshape(flat_count, TOK_DEV, state_width)
    log_blocks = log_decay.reshape(seq_count, head_count, blocks, TOK_DEV).transpose(0, 2, 1, 3).reshape(flat_count, head_count, TOK_DEV)
    reset_blocks = resets.reshape(flat_count, TOK_DEV)

    def prepare(items):
        local_state, local_adjoint, carry_gain, unused_a, unused_b = prepare_block(*items)
        return (local_state, local_adjoint, carry_gain)
    local_states, local_adjoints, gains = lax.map(prepare, (values_blocks, input_blocks, output_blocks, grads_blocks, log_blocks, reset_blocks))
    states_seq = local_states.reshape(seq_count, blocks, inner_width, state_width).swapaxes(0, 1)
    adjoints_seq = local_adjoints.reshape(seq_count, blocks, inner_width, state_width).swapaxes(0, 1)
    gains_seq = gains.reshape(seq_count, blocks, head_count).swapaxes(0, 1)

    def advance(running, element):
        factor, addend = element
        return (jnp.repeat(factor, head_dim, axis=1)[:, :, None] * running + addend, running)
    anchor = jnp.zeros((seq_count, inner_width, state_width), jnp.float32)
    unused_c, state_prefix = lax.scan(advance, anchor, (gains_seq, states_seq))
    unused_d, adjoint_prefix = lax.scan(advance, anchor, (gains_seq, adjoints_seq), reverse=True)
    state_blocks = state_prefix.swapaxes(0, 1).reshape(flat_count, inner_width, state_width)
    adjoint_blocks = adjoint_prefix.swapaxes(0, 1).reshape(flat_count, inner_width, state_width)

    def finish(items):
        return finish_block(items[0], items[1], items[2], items[3], items[4], items[5], skip_gain, items[6], items[7])
    results = lax.map(finish, (values_blocks, input_blocks, output_blocks, grads_blocks, log_blocks, reset_blocks, state_blocks, adjoint_blocks))
    mixed_out = results[0].reshape(seq_count, token_count, inner_width)
    values_grad = results[1].reshape(seq_count, token_count, inner_width)
    input_grad = results[2].reshape(seq_count, token_count, state_width) * (1.0 / jnp.sqrt(jnp.float32(head_count * head_dim)))
    output_scale = jnp.sqrt(jnp.float32(state_width) / jnp.float32(head_count * head_dim * token_count))
    output_grad = results[3].reshape(seq_count, token_count, state_width) * output_scale
    decay_scale = 1.0 / jnp.sqrt(jnp.float32(head_dim * token_count))
    decay_grad = results[4].reshape(seq_count, blocks, head_count, TOK_DEV).transpose(0, 2, 1, 3).reshape(seq_count, head_count, token_count) * decay_scale
    skip_grad = lax.optimization_barrier(jnp.sum(results[5], axis=0)) / jnp.sqrt(jnp.float32(seq_count * token_count * head_dim))
    return (mixed_out, values_grad, input_grad, output_grad, decay_grad, skip_grad)
```

```python
import functools

import jax
import jax.numpy as jnp
from jax import lax
from jax.experimental import pallas as pl
from jax.experimental.pallas import tpu as pltpu
from jax.sharding import Mesh
from jax.sharding import PartitionSpec as P

SEQ = ("seq_0", "seq_1", "seq_2")
CHIPS = ("seq_0", "seq_1")
CORE = "seq_2"
F32 = jnp.float32
BF16 = jnp.bfloat16
T = 128
N = 128
PAIRS = 16
HEADS = 32
DOCS = 8
EXT = 8
FAR = -1e30
VMEM = pl.BlockSpec(memory_space=pltpu.VMEM)
SMEM = pl.BlockSpec(memory_space=pltpu.SMEM)

NN = (((1,), (0,)), ((), ()))
NT = (((1,), (1,)), ((), ()))
TN = (((0,), (0,)), ((), ()))


def dot(a, b, dims=NN, precision=None):
    return lax.dot_general(a, b, dims, precision=precision, preferred_element_type=F32)


def exact(a, b, dims=NN):
    return dot(a, b, dims, lax.Precision.HIGHEST)


def iota(shape, dim):
    return lax.broadcasted_iota(jnp.int32, shape, dim)


def block_base():
    return lax.axis_index(SEQ) * T


def doc_starts(len_ref):
    starts, at = [], jnp.int32(0)
    for d in range(DOCS):
        starts.append(at)
        at = at + len_ref[0, d]
    return starts


def segments(starts, base, offset):
    count = jnp.zeros(offset.shape, jnp.int32)
    for s in starts:
        local = jnp.where(s >= base, s - base, jnp.int32(1 << 20))
        count = count + (offset >= local).astype(jnp.int32)
    return count


def end_count(starts, base):
    count = jnp.int32(0)
    for s in starts:
        count = count + jnp.logical_and(s >= base, s < base + T).astype(jnp.int32)
    return count


def lower_triangle():
    return (iota((T, T), 1) <= iota((T, T), 0)).astype(F32)


def weights(ld, starts, base):
    log_cum = exact(lower_triangle(), ld, NT)
    seg = segments(starts, base, iota((T, HEADS), 0))
    last = end_count(starts, base)
    log_end = log_cum[T - 1 :, :]
    w_end = jnp.where(seg == last, jnp.exp(log_end - log_cum), 0.0)
    w_start = jnp.where(seg == 0, jnp.exp(log_cum), 0.0)
    gain = jnp.exp(log_end) * (last == 0).astype(F32)
    return log_cum, w_end, w_start, gain


def spread(w, j, low):
    return jnp.where(low, w[:, 2 * j : 2 * j + 1], w[:, 2 * j + 1 : 2 * j + 2])


def cols(j):
    return slice(j * 128, (j + 1) * 128)


def prep_kernel(len_ref, v_ref, g_ref, b_ref, c_ref, ld_ref, send_ref, mine_ref, ext_ref):
    first = lax.axis_index(CORE) == 0
    base = block_base()
    starts = doc_starts(len_ref)
    _, w_end, w_start, gain = weights(ld_ref[0], starts, base)
    b_t = b_ref[0].T
    c_t = c_ref[0].T
    low = iota((T, 128), 1) < 64
    sub = iota((EXT, 128), 0)
    skip_rows = []
    for j in range(PAIRS):
        v = v_ref[0, :, cols(j)].astype(F32)
        g = g_ref[0, :, cols(j)].astype(F32)
        wv = (v * spread(w_end, j, low)).astype(BF16)
        wg = (g * spread(w_start, j, low)).astype(BF16)
        state = dot(b_t, wv)
        adjoint = dot(c_t, wg)
        mine_ref[j] = jnp.where(first, state, adjoint)
        send_ref[j, :N] = jnp.where(first, adjoint, state)
        skip_rows.append(jnp.sum(v * g, axis=0, keepdims=True))
    skips = jnp.concatenate(skip_rows, axis=0)
    lane = iota((PAIRS, 128), 1)
    row = iota((PAIRS, 128), 0)
    even = jnp.sum(jnp.where(lane < 64, skips, 0.0), axis=1, keepdims=True)
    odd = jnp.sum(jnp.where(lane < 64, 0.0, skips), axis=1, keepdims=True)
    placed = jnp.where(lane == 2 * row, even, jnp.where(lane == 2 * row + 1, odd, 0.0))
    skip = jnp.sum(placed, axis=0, keepdims=True)
    for j in range(PAIRS):
        gain_row = spread(gain, j, low[:1])
        ext = jnp.where(sub == 0, gain_row, jnp.where(sub == 1, skip, 0.0))
        send_ref[j, N:] = ext
        ext_ref[j] = ext


def combine_kernel(recv_ref, mine_ref, ext_ref, out_ref):
    sub = iota((EXT, 128), 0)
    for j in range(PAIRS):
        theirs = recv_ref[j, N:]
        ours = ext_ref[j]
        out_ref[j, :N] = theirs[:1] * mine_ref[j] + recv_ref[j, :N]
        out_ref[j, N:] = jnp.where(sub == 0, theirs * ours, theirs + ours)


def scan_kernel(in_ref, out_ref, skip_ref):
    first = lax.axis_index(CORE) == 0
    running = jnp.zeros((N, 128), F32)
    skip = jnp.zeros((EXT, 128), F32)
    for i in range(PAIRS):
        at = jnp.where(first, i, PAIRS - 1 - i)
        out_ref[at] = running
        if i < PAIRS - 1:
            running = in_ref[at, N : N + 1] * running + in_ref[at, :N]
        skip = skip + in_ref[i, N:]
    skip_ref[...] = skip


def inside_kernel(len_ref, v_ref, g_ref, b_ref, c_ref, ld_ref, out_ref, back_ref, iraw_ref, oraw_ref):
    base = block_base()
    starts = doc_starts(len_ref)
    tri = lower_triangle()
    ld = ld_ref[0]
    cum_t = exact(tri, ld, NT)
    cum_h = exact(ld, tri, NT)
    t_at = iota((T, T), 0)
    s_at = iota((T, T), 1)
    same = segments(starts, base, t_at) == segments(starts, base, s_at)
    bias = jnp.where(jnp.logical_and(s_at <= t_at, same), 0.0, FAR)
    b = b_ref[0]
    c = c_ref[0]
    scores = dot(c, b, NT)
    low = iota((T, 128), 1) < 64
    zero = jnp.zeros((T, 128), BF16)
    grad_scores = jnp.zeros((T, T), F32)
    for j in range(PAIRS):
        v = v_ref[0, :, cols(j)]
        g = g_ref[0, :, cols(j)]
        v_two = jnp.concatenate([jnp.where(low, v, zero), jnp.where(low, zero, v)], axis=0)
        g_two = jnp.concatenate([jnp.where(low, g, zero), jnp.where(low, zero, g)], axis=0)
        grad_mix = dot(g, v_two, NT)
        mixes = []
        for k in range(2):
            h = 2 * j + k
            decay = jnp.exp(cum_t[:, h : h + 1] - cum_h[h : h + 1, :] + bias)
            mixes.append((scores * decay).astype(BF16))
            grad_scores = grad_scores + grad_mix[:, k * T : (k + 1) * T] * decay
        out_ref[:, cols(j)] = dot(jnp.concatenate(mixes, axis=1), v_two)
        back_ref[:, cols(j)] = dot(jnp.concatenate(mixes, axis=0), g_two, TN)
    half = grad_scores.astype(BF16)
    iraw_ref[...] = dot(half, c, TN)
    oraw_ref[...] = dot(half, b)


def pass_on_kernel(x_ref, mine_ref, ext_ref, out_ref):
    for j in range(PAIRS):
        out_ref[j] = ext_ref[j, :1] * x_ref[j] + mine_ref[j]


def finish_kernel(
    scales,
    len_ref,
    skip_ref,
    v_ref,
    g_ref,
    b_ref,
    c_ref,
    ld_ref,
    x_ref,
    y_ref,
    within_ref,
    back_ref,
    iraw_ref,
    oraw_ref,
    mixed_ref,
    vgrad_ref,
    igrad_ref,
    ograd_ref,
    dgrad_ref,
):
    in_scale, out_scale, decay_scale = scales
    first = lax.axis_index(CORE) == 0
    base = block_base()
    starts = doc_starts(len_ref)
    _, w_end, w_start, gain = weights(ld_ref[0], starts, base)
    b = b_ref[0]
    c = c_ref[0]
    low = iota((T, 128), 1) < 64
    iraw = iraw_ref[...]
    oraw = oraw_ref[...]
    cum_grad = jnp.zeros((T, 128), F32)
    ends = jnp.zeros((1, 128), F32)
    lane = iota((128, 128), 0)
    head = iota((128, 128), 1)
    for j in range(PAIRS):
        x = x_ref[j]
        y = y_ref[j]
        state = jnp.where(first, x, y)
        adjoint = jnp.where(first, y, x)
        state_half = state.astype(BF16)
        adjoint_half = adjoint.astype(BF16)
        v16 = v_ref[0, :, cols(j)]
        g16 = g_ref[0, :, cols(j)]
        v = v16.astype(F32)
        g = g16.astype(F32)
        we = spread(w_end, j, low)
        ws = spread(w_start, j, low)
        skip = jnp.where(low[:1], skip_ref[2 * j], skip_ref[2 * j + 1])
        out = within_ref[:, cols(j)] + ws * dot(c, state_half)
        tail = we * dot(b, adjoint_half)
        back = back_ref[:, cols(j)] + tail
        mixed_ref[0, :, cols(j)] = (out + skip * v).astype(BF16)
        vgrad_ref[0, :, cols(j)] = (back + skip * g).astype(BF16)
        iraw = iraw + dot((v * we).astype(BF16), adjoint_half, NT)
        oraw = oraw + dot((g * ws).astype(BF16), state_half, NT)
        change = g * out - v * back
        gain_row = spread(gain, j, low[:1])
        end = jnp.sum(v * tail, axis=0, keepdims=True) + gain_row * jnp.sum(
            state * adjoint, axis=0, keepdims=True
        )
        change = jnp.where(iota((T, 128), 0) == T - 1, change + end, change)
        pick = (head == 2 * j + jnp.where(lane < 64, 0, 1)).astype(BF16)
        hi = change.astype(BF16)
        lo = (change - hi.astype(F32)).astype(BF16)
        cum_grad = cum_grad + dot(hi, pick) + dot(lo, pick)
    igrad_ref[0] = iraw * in_scale
    ograd_ref[0] = oraw * out_scale
    upper = (iota((T, T), 1) <= iota((T, T), 0)).astype(F32)
    total = exact(cum_grad, upper, TN)[:HEADS]
    offset = iota((HEADS, T), 1)
    reset = jnp.zeros((HEADS, T), jnp.bool_)
    for s in starts:
        reset = jnp.logical_or(reset, offset + base == s)
    dgrad_ref[0] = jnp.where(reset, 0.0, total * decay_scale)


def call(kernel, outs, *args, scalars=0, flops=0, moved=0):
    return pl.pallas_call(
        kernel,
        out_shape=outs,
        in_specs=[SMEM] * scalars + [VMEM] * (len(args) - scalars),
        out_specs=jax.tree.map(lambda _: VMEM, outs),
        cost_estimate=pl.CostEstimate(flops=flops, bytes_accessed=moved, transcendentals=0),
    )(*args)


def f32(*shape):
    return jax.ShapeDtypeStruct(shape, F32)


def swap_cores(x):
    return lax.ppermute(x, CORE, [(0, 1), (1, 0)])


def body(values_in, input_proj, output_proj, log_decay, doc_lengths, skip_gain, out_cotangent):
    inputs = (doc_lengths, values_in, out_cotangent, input_proj, output_proj, log_decay)
    shards = lax.axis_size(SEQ)
    seq_count = lax.axis_size("dp")
    token_count = shards * T
    inner = values_in.shape[2]
    head_dim = inner // HEADS
    send, mine, ext = call(
        prep_kernel,
        (f32(PAIRS, N + EXT, 128), f32(PAIRS, N, 128), f32(PAIRS, EXT, 128)),
        *inputs,
        scalars=1,
        flops=2 * 2 * T * N * inner,
        moved=4 << 20,
    )
    recv = swap_cores(send)
    chip = call(combine_kernel, f32(PAIRS, N + EXT, 128), recv, mine, ext, moved=3 << 20)
    gathered = lax.all_to_all(chip, CHIPS, split_axis=0, concat_axis=0, tiled=True)
    within, back, iraw, oraw = call(
        inside_kernel,
        (f32(T, inner), f32(T, inner), f32(T, N), f32(T, N)),
        *inputs,
        scalars=1,
        flops=40 * 2 * T * N * inner,
        moved=20 << 20,
    )
    prefix, skip = call(
        scan_kernel, (f32(PAIRS, N, 128), f32(EXT, 128)), gathered, moved=2 << 20
    )
    x = lax.all_to_all(prefix, CHIPS, split_axis=0, concat_axis=0, tiled=True)
    for step in (1, 2, 4):
        skip = skip + lax.ppermute(skip, "dp", [(i, i ^ step) for i in range(8)])
    y = swap_cores(call(pass_on_kernel, f32(PAIRS, N, 128), x, mine, ext, moved=3 << 20))
    scales = (
        float(1.0 / inner**0.5),
        float((N / (inner * token_count)) ** 0.5),
        float(1.0 / (head_dim * token_count) ** 0.5),
    )
    mixed, values_grad, input_grad, output_grad, decay_grad = call(
        functools.partial(finish_kernel, scales),
        (
            jax.ShapeDtypeStruct((1, T, inner), BF16),
            jax.ShapeDtypeStruct((1, T, inner), BF16),
            f32(1, T, N),
            f32(1, T, N),
            f32(1, HEADS, T),
        ),
        doc_lengths,
        skip_gain,
        *inputs[1:],
        x,
        y,
        within,
        back,
        iraw,
        oraw,
        scalars=2,
        flops=4 * 2 * T * N * inner,
        moved=8 << 20,
    )
    skip_grad = skip[1, :HEADS] * (1.0 / (seq_count * token_count * head_dim) ** 0.5)
    return mixed, values_grad, input_grad, output_grad, decay_grad, skip_grad


def solution(mesh):
    finer = Mesh(mesh.devices.reshape(mesh.shape["dp"], 4, 4, 2), ("dp",) + SEQ)
    placed = (
        P("dp", SEQ, None),
        P("dp", SEQ, None),
        P("dp", SEQ, None),
        P("dp", None, SEQ),
        P("dp", None),
        P(),
        P("dp", SEQ, None),
    )
    return jax.shard_map(
        body,
        mesh=finer,
        in_specs=placed,
        out_specs=(
            P("dp", SEQ, None),
            P("dp", SEQ, None),
            P("dp", SEQ, None),
            P("dp", SEQ, None),
            P("dp", None, SEQ),
            P(),
        ),
        check_vma=False,
    )
```

```python
import functools

import jax
import jax.numpy as jnp
from jax import lax
from jax.experimental import pallas as pl
from jax.experimental.pallas import tpu as pltpu
from jax.sharding import Mesh
from jax.sharding import PartitionSpec as P

SEQ = ("seq_0", "seq_1", "seq_2")
CHIPS = ("seq_0", "seq_1")
CORE = "seq_2"
F32 = jnp.float32
BF16 = jnp.bfloat16
T = 128
N = 128
PAIRS = 16
HEADS = 32
DOCS = 8
EXT = 8
FAR = -1e30
VMEM = pl.BlockSpec(memory_space=pltpu.VMEM)
SMEM = pl.BlockSpec(memory_space=pltpu.SMEM)
ANY = pl.BlockSpec(memory_space=pl.ANY)
HBM = pl.BlockSpec(memory_space=pltpu.HBM)

NN = (((1,), (0,)), ((), ()))
NT = (((1,), (1,)), ((), ()))
TN = (((0,), (0,)), ((), ()))


def dot(a, b, dims=NN, precision=None):
    return lax.dot_general(a, b, dims, precision=precision, preferred_element_type=F32)


def exact(a, b, dims=NN):
    return dot(a, b, dims, lax.Precision.HIGHEST)


def iota(shape, dim):
    return lax.broadcasted_iota(jnp.int32, shape, dim)


def block_base():
    return lax.axis_index(SEQ) * T


def doc_starts(len_ref):
    starts, at = [], jnp.int32(0)
    for d in range(DOCS):
        starts.append(at)
        at = at + len_ref[0, d]
    return starts


def segments(starts, base, offset):
    count = jnp.zeros(offset.shape, jnp.int32)
    for s in starts:
        local = jnp.where(s >= base, s - base, jnp.int32(1 << 20))
        count = count + (offset >= local).astype(jnp.int32)
    return count


def end_count(starts, base):
    count = jnp.int32(0)
    for s in starts:
        count = count + jnp.logical_and(s >= base, s < base + T).astype(jnp.int32)
    return count


def lower_triangle():
    return (iota((T, T), 1) <= iota((T, T), 0)).astype(F32)


def weights(ld, starts, base):
    log_cum = exact(lower_triangle(), ld, NT)
    seg = segments(starts, base, iota((T, HEADS), 0))
    last = end_count(starts, base)
    log_end = log_cum[T - 1 :, :]
    w_end = jnp.where(seg == last, jnp.exp(log_end - log_cum), 0.0)
    w_start = jnp.where(seg == 0, jnp.exp(log_cum), 0.0)
    gain = jnp.exp(log_end) * (last == 0).astype(F32)
    return log_cum, w_end, w_start, gain


def spread(w, j, low):
    return jnp.where(low, w[:, 2 * j : 2 * j + 1], w[:, 2 * j + 1 : 2 * j + 2])


def cols(j):
    return slice(j * 128, (j + 1) * 128)


def prep_kernel(len_ref, v_ref, g_ref, b_ref, c_ref, ld_ref, send_ref, mine_ref, ext_ref):
    first = lax.axis_index(CORE) == 0
    base = block_base()
    starts = doc_starts(len_ref)
    _, w_end, w_start, gain = weights(ld_ref[0], starts, base)
    b_t = b_ref[0].T
    c_t = c_ref[0].T
    low = iota((T, 128), 1) < 64
    sub = iota((EXT, 128), 0)
    skip_rows = []
    for j in range(PAIRS):
        v = v_ref[0, :, cols(j)].astype(F32)
        g = g_ref[0, :, cols(j)].astype(F32)
        wv = (v * spread(w_end, j, low)).astype(BF16)
        wg = (g * spread(w_start, j, low)).astype(BF16)
        state = dot(b_t, wv)
        adjoint = dot(c_t, wg)
        mine_ref[j] = jnp.where(first, state, adjoint)
        send_ref[j, :N] = jnp.where(first, adjoint, state)
        skip_rows.append(jnp.sum(v * g, axis=0, keepdims=True))
    skips = jnp.concatenate(skip_rows, axis=0)
    lane = iota((PAIRS, 128), 1)
    row = iota((PAIRS, 128), 0)
    even = jnp.sum(jnp.where(lane < 64, skips, 0.0), axis=1, keepdims=True)
    odd = jnp.sum(jnp.where(lane < 64, 0.0, skips), axis=1, keepdims=True)
    placed = jnp.where(lane == 2 * row, even, jnp.where(lane == 2 * row + 1, odd, 0.0))
    skip = jnp.sum(placed, axis=0, keepdims=True)
    for j in range(PAIRS):
        gain_row = spread(gain, j, low[:1])
        ext = jnp.where(sub == 0, gain_row, jnp.where(sub == 1, skip, 0.0))
        send_ref[j, N:] = ext
        ext_ref[j] = ext


def put(buffer, out_ref, sems, j):
    return pltpu.make_async_copy(buffer.at[j], out_ref.at[j], sems.at[j])


def combine_kernel(recv_ref, mine_ref, ext_ref, out_ref, buffer, sems):
    sub = iota((EXT, 128), 0)
    copies = []
    for j in range(PAIRS):
        theirs = recv_ref[j, N:]
        ours = ext_ref[j]
        buffer[j, :N] = theirs[:1] * mine_ref[j] + recv_ref[j, :N]
        buffer[j, N:] = jnp.where(sub == 0, theirs * ours, theirs + ours)
        copies.append(put(buffer, out_ref, sems, j))
        copies[-1].start()
    for copy in copies:
        copy.wait()


def scan_kernel(_, in_ref, skip_ref, out_ref, buffer, sems):
    first = lax.axis_index(CORE) == 0
    running = jnp.zeros((N, 128), F32)
    skip = jnp.zeros((EXT, 128), F32)
    copies = []
    for i in range(PAIRS):
        at = jnp.where(first, i, PAIRS - 1 - i)
        buffer[i] = running
        copies.append(pltpu.make_async_copy(buffer.at[i], out_ref.at[at], sems.at[i]))
        copies[-1].start()
        if i < PAIRS - 1:
            running = in_ref[at, N : N + 1] * running + in_ref[at, :N]
        skip = skip + in_ref[i, N:]
    skip_ref[...] = skip
    for copy in copies:
        copy.wait()


def inside_kernel(_, len_ref, v_ref, g_ref, b_ref, c_ref, ld_ref, out_ref, back_ref, iraw_ref, oraw_ref):
    base = block_base()
    starts = doc_starts(len_ref)
    tri = lower_triangle()
    ld = ld_ref[0]
    cum_t = exact(tri, ld, NT)
    cum_h = exact(ld, tri, NT)
    t_at = iota((T, T), 0)
    s_at = iota((T, T), 1)
    same = segments(starts, base, t_at) == segments(starts, base, s_at)
    bias = jnp.where(jnp.logical_and(s_at <= t_at, same), 0.0, FAR)
    b = b_ref[0]
    c = c_ref[0]
    scores = dot(c, b, NT)
    low = iota((T, 128), 1) < 64
    zero = jnp.zeros((T, 128), BF16)
    grad_scores = jnp.zeros((T, T), F32)
    for j in range(PAIRS):
        v = v_ref[0, :, cols(j)]
        g = g_ref[0, :, cols(j)]
        v_two = jnp.concatenate([jnp.where(low, v, zero), jnp.where(low, zero, v)], axis=0)
        g_two = jnp.concatenate([jnp.where(low, g, zero), jnp.where(low, zero, g)], axis=0)
        grad_mix = dot(g, v_two, NT)
        mixes = []
        for k in range(2):
            h = 2 * j + k
            decay = jnp.exp(cum_t[:, h : h + 1] - cum_h[h : h + 1, :] + bias)
            mixes.append((scores * decay).astype(BF16))
            grad_scores = grad_scores + grad_mix[:, k * T : (k + 1) * T] * decay
        out_ref[:, cols(j)] = dot(jnp.concatenate(mixes, axis=1), v_two)
        back_ref[:, cols(j)] = dot(jnp.concatenate(mixes, axis=0), g_two, TN)
    half = grad_scores.astype(BF16)
    iraw_ref[...] = dot(half, c, TN)
    oraw_ref[...] = dot(half, b)


def pass_on_kernel(_, x_ref, mine_ref, ext_ref, out_ref):
    for j in range(PAIRS):
        out_ref[j] = ext_ref[j, :1] * x_ref[j] + mine_ref[j]


def finish_kernel(
    scales,
    len_ref,
    skip_ref,
    v_ref,
    g_ref,
    b_ref,
    c_ref,
    ld_ref,
    x_ref,
    y_ref,
    within_ref,
    back_ref,
    iraw_ref,
    oraw_ref,
    mixed_ref,
    vgrad_ref,
    igrad_ref,
    ograd_ref,
    dgrad_ref,
):
    in_scale, out_scale, decay_scale = scales
    first = lax.axis_index(CORE) == 0
    base = block_base()
    starts = doc_starts(len_ref)
    _, w_end, w_start, gain = weights(ld_ref[0], starts, base)
    b = b_ref[0]
    c = c_ref[0]
    low = iota((T, 128), 1) < 64
    iraw = iraw_ref[...]
    oraw = oraw_ref[...]
    cum_grad = jnp.zeros((T, 128), F32)
    ends = jnp.zeros((1, 128), F32)
    lane = iota((128, 128), 0)
    head = iota((128, 128), 1)
    for j in range(PAIRS):
        x = x_ref[j]
        y = y_ref[j]
        state = jnp.where(first, x, y)
        adjoint = jnp.where(first, y, x)
        state_half = state.astype(BF16)
        adjoint_half = adjoint.astype(BF16)
        v16 = v_ref[0, :, cols(j)]
        g16 = g_ref[0, :, cols(j)]
        v = v16.astype(F32)
        g = g16.astype(F32)
        we = spread(w_end, j, low)
        ws = spread(w_start, j, low)
        skip = jnp.where(low[:1], skip_ref[2 * j], skip_ref[2 * j + 1])
        out = within_ref[:, cols(j)] + ws * dot(c, state_half)
        tail = we * dot(b, adjoint_half)
        back = back_ref[:, cols(j)] + tail
        mixed_ref[0, :, cols(j)] = (out + skip * v).astype(BF16)
        vgrad_ref[0, :, cols(j)] = (back + skip * g).astype(BF16)
        iraw = iraw + dot((v * we).astype(BF16), adjoint_half, NT)
        oraw = oraw + dot((g * ws).astype(BF16), state_half, NT)
        change = g * out - v * back
        gain_row = spread(gain, j, low[:1])
        end = jnp.sum(v * tail, axis=0, keepdims=True) + gain_row * jnp.sum(
            state * adjoint, axis=0, keepdims=True
        )
        change = jnp.where(iota((T, 128), 0) == T - 1, change + end, change)
        pick = (head == 2 * j + jnp.where(lane < 64, 0, 1)).astype(BF16)
        hi = change.astype(BF16)
        lo = (change - hi.astype(F32)).astype(BF16)
        cum_grad = cum_grad + dot(hi, pick) + dot(lo, pick)
    igrad_ref[0] = iraw * in_scale
    ograd_ref[0] = oraw * out_scale
    upper = (iota((T, T), 1) <= iota((T, T), 0)).astype(F32)
    total = exact(cum_grad, upper, TN)[:HEADS]
    offset = iota((HEADS, T), 1)
    reset = jnp.zeros((HEADS, T), jnp.bool_)
    for s in starts:
        reset = jnp.logical_or(reset, offset + base == s)
    dgrad_ref[0] = jnp.where(reset, 0.0, total * decay_scale)


def call(kernel, outs, *args, after=(), scalars=0, flops=0, moved=0, limit=16, staged=False):
    args = tuple(after) + args
    free = len(after)
    out_specs = [VMEM] * len(outs)
    scratch = []
    if staged:
        out_specs[-1] = HBM
        scratch = [pltpu.VMEM(outs[-1].shape, F32), pltpu.SemaphoreType.DMA((PAIRS,))]
    return pl.pallas_call(
        kernel,
        out_shape=outs,
        in_specs=[ANY] * free + [SMEM] * scalars + [VMEM] * (len(args) - scalars - free),
        out_specs=out_specs,
        scratch_shapes=scratch,
        compiler_params=pltpu.CompilerParams(vmem_limit_bytes=limit << 20),
        cost_estimate=pl.CostEstimate(flops=flops, bytes_accessed=moved, transcendentals=0),
    )(*args)


def f32(*shape):
    return jax.ShapeDtypeStruct(shape, F32)


def swap_cores(x):
    return lax.ppermute(x, CORE, [(0, 1), (1, 0)])


def body(values_in, input_proj, output_proj, log_decay, doc_lengths, skip_gain, out_cotangent):
    inputs = (doc_lengths, values_in, out_cotangent, input_proj, output_proj, log_decay)
    shards = lax.axis_size(SEQ)
    seq_count = lax.axis_size("dp")
    token_count = shards * T
    inner = values_in.shape[2]
    head_dim = inner // HEADS
    send, mine, ext = call(
        prep_kernel,
        (f32(PAIRS, N + EXT, 128), f32(PAIRS, N, 128), f32(PAIRS, EXT, 128)),
        *inputs,
        scalars=1,
        flops=2 * 2 * T * N * inner,
        moved=4 << 20,
    )
    recv = swap_cores(send)
    (chip,) = call(
        combine_kernel, (f32(PAIRS, N + EXT, 128),), recv, mine, ext, moved=3 << 20, staged=True
    )
    gathered = lax.all_to_all(chip, CHIPS, split_axis=0, concat_axis=0, tiled=True)
    within, back, iraw, oraw = call(
        inside_kernel,
        (f32(T, inner), f32(T, inner), f32(T, N), f32(T, N)),
        *inputs,
        after=(chip,),
        scalars=1,
        flops=40 * 2 * T * N * inner,
        moved=20 << 20,
    )
    skip, prefix = call(
        scan_kernel,
        (f32(EXT, 128), f32(PAIRS, N, 128)),
        gathered,
        after=(iraw,),
        moved=2 << 20,
        staged=True,
    )
    x = lax.all_to_all(prefix, CHIPS, split_axis=0, concat_axis=0, tiled=True)
    for step in (1, 2, 4):
        skip = skip + lax.ppermute(skip, "dp", [(i, i ^ step) for i in range(8)])
    (passed,) = call(
        pass_on_kernel, (f32(PAIRS, N, 128),), x, mine, ext, after=(skip,), moved=3 << 20
    )
    y = swap_cores(passed)
    scales = (
        float(1.0 / inner**0.5),
        float((N / (inner * token_count)) ** 0.5),
        float(1.0 / (head_dim * token_count) ** 0.5),
    )
    mixed, values_grad, input_grad, output_grad, decay_grad = call(
        functools.partial(finish_kernel, scales),
        (
            jax.ShapeDtypeStruct((1, T, inner), BF16),
            jax.ShapeDtypeStruct((1, T, inner), BF16),
            f32(1, T, N),
            f32(1, T, N),
            f32(1, HEADS, T),
        ),
        doc_lengths,
        skip_gain,
        *inputs[1:],
        x,
        y,
        within,
        back,
        iraw,
        oraw,
        scalars=2,
        flops=4 * 2 * T * N * inner,
        moved=8 << 20,
    )
    skip_grad = skip[1, :HEADS] * (1.0 / (seq_count * token_count * head_dim) ** 0.5)
    return mixed, values_grad, input_grad, output_grad, decay_grad, skip_grad


def solution(mesh):
    finer = Mesh(mesh.devices.reshape(mesh.shape["dp"], 4, 4, 2), ("dp",) + SEQ)
    placed = (
        P("dp", SEQ, None),
        P("dp", SEQ, None),
        P("dp", SEQ, None),
        P("dp", None, SEQ),
        P("dp", None),
        P(),
        P("dp", SEQ, None),
    )
    return jax.shard_map(
        body,
        mesh=finer,
        in_specs=placed,
        out_specs=(
            P("dp", SEQ, None),
            P("dp", SEQ, None),
            P("dp", SEQ, None),
            P("dp", SEQ, None),
            P("dp", None, SEQ),
            P(),
        ),
        check_vma=False,
    )
```

```python
import functools

import jax
import jax.numpy as jnp
from jax import lax
from jax.experimental import pallas as pl
from jax.experimental.pallas import tpu as pltpu
from jax.sharding import Mesh
from jax.sharding import PartitionSpec as P

SEQ = ("seq_0", "seq_1", "seq_2")
CHIPS = ("seq_0", "seq_1")
CORE = "seq_2"
F32 = jnp.float32
BF16 = jnp.bfloat16
T = 128
N = 128
PAIRS = 16
HEADS = 32
DOCS = 8
EXT = 8
PARTS = 4
PART = 512
FAR = -1e30
VMEM = pl.BlockSpec(memory_space=pltpu.VMEM)
SMEM = pl.BlockSpec(memory_space=pltpu.SMEM)
ANY = pl.BlockSpec(memory_space=pl.ANY)
HBM = pl.BlockSpec(memory_space=pltpu.HBM)

NN = (((1,), (0,)), ((), ()))
NT = (((1,), (1,)), ((), ()))
TN = (((0,), (0,)), ((), ()))


def dot(a, b, dims=NN, precision=None):
    return lax.dot_general(a, b, dims, precision=precision, preferred_element_type=F32)


def exact(a, b, dims=NN):
    return dot(a, b, dims, lax.Precision.HIGHEST)


def iota(shape, dim):
    return lax.broadcasted_iota(jnp.int32, shape, dim)


def block_base():
    return lax.axis_index(SEQ) * T


def doc_starts(len_ref):
    starts, at = [], jnp.int32(0)
    for d in range(DOCS):
        starts.append(at)
        at = at + len_ref[0, d]
    return starts


def segments(starts, base, offset):
    count = jnp.zeros(offset.shape, jnp.int32)
    for s in starts:
        local = jnp.where(s >= base, s - base, jnp.int32(1 << 20))
        count = count + (offset >= local).astype(jnp.int32)
    return count


def end_count(starts, base):
    count = jnp.int32(0)
    for s in starts:
        count = count + jnp.logical_and(s >= base, s < base + T).astype(jnp.int32)
    return count


def lower_triangle():
    return (iota((T, T), 1) <= iota((T, T), 0)).astype(F32)


def weights(ld, starts, base):
    log_cum = exact(lower_triangle(), ld, NT)
    seg = segments(starts, base, iota((T, HEADS), 0))
    last = end_count(starts, base)
    log_end = log_cum[T - 1 :, :]
    w_end = jnp.where(seg == last, jnp.exp(log_end - log_cum), 0.0)
    w_start = jnp.where(seg == 0, jnp.exp(log_cum), 0.0)
    gain = jnp.exp(log_end) * (last == 0).astype(F32)
    return w_end, w_start, gain


def spread(w, j, low):
    return jnp.where(low, w[:, 2 * j : 2 * j + 1], w[:, 2 * j + 1 : 2 * j + 2])


def cols(j):
    return slice(j * 128, (j + 1) * 128)


def heads_of(rows):
    lane = iota((PAIRS, 128), 1)
    row = iota((PAIRS, 128), 0)
    even = jnp.sum(jnp.where(lane < 64, rows, 0.0), axis=1, keepdims=True)
    odd = jnp.sum(jnp.where(lane < 64, 0.0, rows), axis=1, keepdims=True)
    placed = jnp.where(lane == 2 * row, even, jnp.where(lane == 2 * row + 1, odd, 0.0))
    return jnp.sum(placed, axis=0, keepdims=True)


def is_first():
    return lax.axis_index(CORE) == 0


def prep_kernel(
    len_hbm, v_hbm, g_hbm, b_hbm, c_hbm, ld_hbm,
    roles_ref, rows_ref, w_ref, gain_ref, send_ref,
    len_ref, ld_ref, small_sems, v_sems, g_sems,
):
    first = is_first()
    v_slot = jnp.where(first, 1, 0)
    g_slot = 1 - v_slot
    small = [
        pltpu.make_async_copy(len_hbm, len_ref, small_sems.at[0]),
        pltpu.make_async_copy(ld_hbm.at[0], ld_ref, small_sems.at[1]),
        pltpu.make_async_copy(b_hbm.at[0], rows_ref.at[v_slot], small_sems.at[2]),
        pltpu.make_async_copy(c_hbm.at[0], rows_ref.at[g_slot], small_sems.at[3]),
    ]
    for copy in small:
        copy.start()
    wide = []
    for k in range(PARTS):
        part = slice(k * PART, (k + 1) * PART)
        vc = pltpu.make_async_copy(
            v_hbm.at[0, :, part], roles_ref.at[v_slot, :, part], v_sems.at[k]
        )
        gc = pltpu.make_async_copy(
            g_hbm.at[0, :, part], roles_ref.at[g_slot, :, part], g_sems.at[k]
        )
        vc.start()
        gc.start()
        wide.append((vc, gc))
    for copy in small:
        copy.wait()
    starts = doc_starts(len_ref)
    w_end, w_start, gain = weights(ld_ref[...], starts, block_base())
    w = jnp.where(first, w_start, w_end)
    w_ref[0] = w
    w_ref[1] = jnp.where(first, w_end, w_start)
    p_t = rows_ref[0].T
    low = iota((T, 128), 1) < 64
    sub = iota((EXT, 128), 0)
    for j in range(PAIRS):
        if j % (PAIRS // PARTS) == 0:
            for copy in wide[j // (PAIRS // PARTS)]:
                copy.wait()
        weighted = (roles_ref[0, :, cols(j)].astype(F32) * spread(w, j, low)).astype(BF16)
        send_ref[j, :N] = dot(p_t, weighted)
        gain_row = spread(gain, j, low[:1])
        gain_ref[j : j + 1] = gain_row
        send_ref[j, N:] = jnp.where(sub == 0, gain_row, 0.0)


def own_kernel(
    _, len_ref, skip_gain_ref, roles_ref, rows_ref, w_ref,
    mine_ref, keep_ref, gains_ref, skip_ref,
):
    low = iota((T, 128), 1) < 64
    p_t = rows_ref[1].T
    w = w_ref[1]
    skips = []
    for j in range(PAIRS):
        mine = roles_ref[1, :, cols(j)].astype(F32)
        other = roles_ref[0, :, cols(j)].astype(F32)
        mine_ref[j] = dot(p_t, (mine * spread(w, j, low)).astype(BF16))
        skips.append(jnp.sum(mine * other, axis=0, keepdims=True))
        gains_ref[j : j + 1] = jnp.where(
            low[:1], skip_gain_ref[2 * j], skip_gain_ref[2 * j + 1]
        )
    skip = heads_of(jnp.concatenate(skips, axis=0))
    skip_ref[...] = jnp.broadcast_to(skip, (EXT, 128))
    base = block_base()
    starts = doc_starts(len_ref)
    offset = iota((EXT, T), 1)
    keep = jnp.ones((EXT, T), F32)
    for s in starts:
        keep = jnp.where(offset + base == s, 0.0, keep)
    keep_ref[...] = keep


def put(buffer, out_ref, sems, j):
    return pltpu.make_async_copy(buffer.at[j], out_ref.at[j], sems.at[j])


def combine_kernel(recv_ref, mine_ref, gain_ref, out_ref, buffer, sems):
    copies = []
    for j in range(PAIRS):
        theirs = recv_ref[j, N:]
        buffer[j, :N] = theirs[:1] * mine_ref[j] + recv_ref[j, :N]
        buffer[j, N:] = theirs * gain_ref[j : j + 1]
        copies.append(put(buffer, out_ref, sems, j))
        copies[-1].start()
    for copy in copies:
        copy.wait()


def scan_kernel(in_ref, skip_ref, out_ref, buffer, sems):
    first = is_first()
    running = jnp.zeros((N, 128), F32)
    copies = []
    for i in range(PAIRS):
        at = jnp.where(first, i, PAIRS - 1 - i)
        buffer[i, :N] = running
        buffer[i, N:] = skip_ref[...]
        copies.append(pltpu.make_async_copy(buffer.at[i], out_ref.at[at], sems.at[i]))
        copies[-1].start()
        if i < PAIRS - 1:
            running = in_ref[at, N : N + 1] * running + in_ref[at, :N]
    for copy in copies:
        copy.wait()


def inside_kernel(_, len_ref, roles_ref, rows_ref, ld_ref, part_ref, raw_ref):
    first = is_first()
    v_slot = jnp.where(first, 1, 0)
    g_slot = 1 - v_slot
    base = block_base()
    starts = doc_starts(len_ref)
    ld = ld_ref[0]
    tri = lower_triangle()
    cum_t = exact(tri, ld, NT)
    cum_h = exact(ld, tri, NT)
    t_at = iota((T, T), 0)
    s_at = iota((T, T), 1)
    same = segments(starts, base, t_at) == segments(starts, base, s_at)
    bias = jnp.where(jnp.logical_and(s_at <= t_at, same), 0.0, FAR)
    b = rows_ref[v_slot]
    c = rows_ref[g_slot]
    scores = dot(c, b, NT)
    low = iota((T, 128), 1) < 64
    zero = jnp.zeros((T, 128), BF16)
    grad_scores = jnp.zeros((T, T), F32)
    for j in range(PAIRS):
        v = roles_ref[v_slot, :, cols(j)]
        g = roles_ref[g_slot, :, cols(j)]
        v_two = jnp.concatenate([jnp.where(low, v, zero), jnp.where(low, zero, v)], axis=0)
        g_two = jnp.concatenate([jnp.where(low, g, zero), jnp.where(low, zero, g)], axis=0)
        grad_mix = dot(g, v_two, NT)
        mixes = []
        for k in range(2):
            h = 2 * j + k
            decay = jnp.exp(cum_t[:, h : h + 1] - cum_h[h : h + 1, :] + bias)
            mixes.append((scores * decay).astype(BF16))
            grad_scores = grad_scores + grad_mix[:, k * T : (k + 1) * T] * decay
        part_ref[g_slot, :, cols(j)] = dot(jnp.concatenate(mixes, axis=1), v_two)
        part_ref[v_slot, :, cols(j)] = dot(jnp.concatenate(mixes, axis=0), g_two, TN)
    half = grad_scores.astype(BF16)
    raw_ref[g_slot] = dot(half, b)
    raw_ref[v_slot] = dot(half, c, TN)


def pass_on_kernel(scale, _, x_ref, mine_ref, gain_ref, out_ref, skip_ref):
    skip = x_ref[0, N:]
    for j in range(PAIRS):
        out_ref[j] = gain_ref[j : j + 1] * x_ref[j, :N] + mine_ref[j]
        if j > 0:
            skip = skip + x_ref[j, N:]
    skip_ref[...] = skip * scale


def finish_role(slot, j, low, x, roles_ref, rows, w, part_ref, skip_gains):
    half = x.astype(BF16)
    own = roles_ref[slot, :, cols(j)].astype(F32)
    skipped = roles_ref[1 - slot, :, cols(j)].astype(F32)
    wide = spread(w, j, low)
    tail = wide * dot(rows, half)
    out = part_ref[slot, :, cols(j)] + tail
    result = (out + skip_gains[j : j + 1] * skipped).astype(BF16)
    change = own * out
    hi = change.astype(BF16)
    lo = (change - hi.astype(F32)).astype(BF16)
    lane = iota((128, 128), 0)
    head = iota((128, 128), 1)
    pick = (head == 2 * j + jnp.where(lane < 64, 0, 1)).astype(BF16)
    end = jnp.sum(own * tail, axis=0, keepdims=True)
    return result, dot(hi, pick) + dot(lo, pick), end, dot((own * wide).astype(BF16), half, NT)


def near_kernel(
    _, x_ref, roles_ref, rows_ref, w_ref, part_ref, raw_ref, gains_ref,
    out_ref, total_ref, change_ref, end_ref,
):
    low = iota((T, 128), 1) < 64
    rows = rows_ref[0]
    w = w_ref[0]
    skip_gains = gains_ref[...]
    total = raw_ref[0]
    changes = jnp.zeros((T, 128), F32)
    for j in range(PAIRS):
        result, change, end, more = finish_role(
            0, j, low, x_ref[j, :N], roles_ref, rows, w, part_ref, skip_gains
        )
        out_ref[:, cols(j)] = result
        changes = changes + change
        total = total + more
        end_ref[j : j + 1] = end
    total_ref[...] = total
    change_ref[...] = changes


def far_kernel(
    scales, y_ref, x_ref, roles_ref, rows_ref, w_ref, part_ref, raw_ref, gains_ref,
    gain_ref, keep_ref, near_ref, near_total_ref, near_change_ref, near_end_ref,
    igrad_ref, ograd_ref, dgrad_ref, mixed_hbm, vgrad_hbm,
    mixed_ref, vgrad_ref, sems,
):
    in_scale, out_scale, decay_scale = scales
    first = is_first()
    low = iota((T, 128), 1) < 64
    rows = rows_ref[1]
    w = w_ref[1]
    skip_gains = gains_ref[...]
    total = raw_ref[1]
    changes = near_change_ref[...]
    ends = []
    copies = []
    for j in range(PAIRS):
        y = y_ref[j]
        result, change, end, more = finish_role(
            1, j, low, y, roles_ref, rows, w, part_ref, skip_gains
        )
        near = near_ref[:, cols(j)]
        mixed_ref[:, cols(j)] = jnp.where(first, near, result)
        vgrad_ref[:, cols(j)] = jnp.where(first, result, near)
        if (j + 1) % (PAIRS // PARTS) == 0:
            k = j // (PAIRS // PARTS)
            part = slice(k * PART, (k + 1) * PART)
            for n, (src, dst) in enumerate(((mixed_ref, mixed_hbm), (vgrad_ref, vgrad_hbm))):
                copies.append(
                    pltpu.make_async_copy(src.at[:, part], dst.at[0, :, part], sems.at[n, k])
                )
                copies[-1].start()
        changes = changes - change
        total = total + more
        meet = jnp.sum(x_ref[j, :N] * y, axis=0, keepdims=True)
        end = jnp.where(first, end, near_end_ref[j : j + 1])
        ends.append(end + gain_ref[j : j + 1] * meet)
    near_total = near_total_ref[...]
    igrad_ref[0] = jnp.where(first, total, near_total) * in_scale
    ograd_ref[0] = jnp.where(first, near_total, total) * out_scale
    changes = jnp.where(first, changes, -changes)
    at_end = iota((T, 128), 0) == T - 1
    changes = changes + jnp.where(at_end, heads_of(jnp.concatenate(ends, axis=0)), 0.0)
    summed = exact(changes, lower_triangle(), TN)[:HEADS]
    dgrad_ref[0] = summed * keep_ref[:1] * decay_scale
    for copy in copies:
        copy.wait()


def call(kernel, outs, *args, after=(), spaces=(), out_spaces=(), scratch=(), flops=0, moved=0):
    in_specs = [ANY] * len(after) + list(spaces)
    in_specs += [VMEM] * (len(args) + len(after) - len(in_specs))
    out_specs = [VMEM] * (len(outs) - len(out_spaces)) + list(out_spaces)
    return pl.pallas_call(
        kernel,
        out_shape=tuple(outs),
        in_specs=in_specs,
        out_specs=tuple(out_specs),
        scratch_shapes=list(scratch),
        compiler_params=pltpu.CompilerParams(vmem_limit_bytes=16 << 20),
        cost_estimate=pl.CostEstimate(flops=flops, bytes_accessed=moved, transcendentals=0),
    )(*after, *args)


def f32(*shape):
    return jax.ShapeDtypeStruct(shape, F32)


def bf16(*shape):
    return jax.ShapeDtypeStruct(shape, BF16)


def swap_cores(x):
    return lax.ppermute(x, CORE, [(0, 1), (1, 0)])


def exchange(x):
    return lax.all_to_all(x, CHIPS, split_axis=0, concat_axis=0, tiled=True)


def body(values_in, input_proj, output_proj, log_decay, doc_lengths, skip_gain, out_cotangent):
    token_count = lax.axis_size(SEQ) * T
    seq_count = lax.axis_size("dp")
    inner = values_in.shape[2]
    head_dim = inner // HEADS
    dma = pltpu.SemaphoreType.DMA
    inputs = (doc_lengths, values_in, out_cotangent, input_proj, output_proj, log_decay)
    roles, rows, w, gain, send = call(
        prep_kernel,
        (
            bf16(2, T, inner), bf16(2, T, N), f32(2, T, HEADS), f32(PAIRS, 128),
            f32(PAIRS, N + EXT, 128),
        ),
        *(pltpu.with_memory_space_constraint(a, pltpu.HBM) for a in inputs),
        spaces=[HBM] * 6,
        scratch=[
            pltpu.SMEM((1, DOCS), jnp.int32), pltpu.VMEM((HEADS, T), F32),
            dma((4,)), dma((PARTS,)), dma((PARTS,)),
        ],
        moved=4 << 20,
    )
    recv = swap_cores(send)
    mine, keep, gains, skip = call(
        own_kernel,
        (f32(PAIRS, N, 128), f32(EXT, T), f32(PAIRS, 128), f32(EXT, 128)),
        doc_lengths, skip_gain, roles, rows, w,
        after=(send,),
        spaces=[SMEM] * 2,
        moved=4 << 20,
    )
    (chip,) = call(
        combine_kernel,
        (f32(PAIRS, N + EXT, 128),),
        recv, mine, gain,
        out_spaces=[HBM],
        scratch=[pltpu.VMEM((PAIRS, N + EXT, 128), F32), dma((PAIRS,))],
        moved=3 << 20,
    )
    gathered = exchange(chip)
    skip, _ = lax.optimization_barrier((skip, chip))
    skip = skip + swap_cores(skip)
    for step in (1, 2, 4):
        skip = skip + lax.ppermute(skip, "dp", [(i, i ^ step) for i in range(8)])
    (prefix,) = call(
        scan_kernel,
        (f32(PAIRS, N + EXT, 128),),
        gathered, skip,
        out_spaces=[HBM],
        scratch=[pltpu.VMEM((PAIRS, N + EXT, 128), F32), dma((PAIRS,))],
        moved=2 << 20,
    )
    x = exchange(prefix)
    part, raw = call(
        inside_kernel,
        (f32(2, T, inner), f32(2, T, N)),
        doc_lengths, roles, rows, log_decay,
        after=(prefix,),
        spaces=[SMEM],
        flops=40 * 2 * T * N * inner,
        moved=20 << 20,
    )
    passed, skip_total = call(
        functools.partial(pass_on_kernel, 1.0 / (seq_count * token_count * head_dim) ** 0.5),
        (f32(PAIRS, N, 128), f32(EXT, 128)),
        x, mine, gain,
        after=(raw,),
        moved=3 << 20,
    )
    y = swap_cores(passed)
    near, near_total, near_change, near_end = call(
        near_kernel,
        (bf16(T, inner), f32(T, N), f32(T, 128), f32(PAIRS, 128)),
        x, roles, rows, w, part, raw, gains,
        after=(passed,),
        moved=8 << 20,
    )
    scales = (
        1.0 / inner**0.5,
        (N / (inner * token_count)) ** 0.5,
        1.0 / (head_dim * token_count) ** 0.5,
    )
    input_grad, output_grad, decay_grad, mixed, values_grad = call(
        functools.partial(far_kernel, scales),
        (f32(1, T, N), f32(1, T, N), f32(1, HEADS, T), bf16(1, T, inner), bf16(1, T, inner)),
        y, x, roles, rows, w, part, raw, gains, gain, keep,
        near, near_total, near_change, near_end,
        out_spaces=[HBM] * 2,
        scratch=[pltpu.VMEM((T, inner), BF16), pltpu.VMEM((T, inner), BF16), dma((2, PARTS))],
        moved=8 << 20,
    )
    return mixed, values_grad, input_grad, output_grad, decay_grad, skip_total[1, :HEADS]


def solution(mesh):
    finer = Mesh(mesh.devices.reshape(mesh.shape["dp"], 4, 4, 2), ("dp",) + SEQ)
    placed = (
        P("dp", SEQ, None),
        P("dp", SEQ, None),
        P("dp", SEQ, None),
        P("dp", None, SEQ),
        P("dp", None),
        P(),
        P("dp", SEQ, None),
    )
    return jax.shard_map(
        body,
        mesh=finer,
        in_specs=placed,
        out_specs=(
            P("dp", SEQ, None),
            P("dp", SEQ, None),
            P("dp", SEQ, None),
            P("dp", SEQ, None),
            P("dp", None, SEQ),
            P(),
        ),
        check_vma=False,
    )
```

```python
import functools

import jax
import jax.numpy as jnp
from jax import lax
from jax.experimental import pallas as pl
from jax.experimental.pallas import tpu as pltpu
from jax.sharding import Mesh
from jax.sharding import PartitionSpec as P

SEQ = ("seq_0", "seq_1", "seq_2")
ROW, COL = "seq_0", "seq_1"
CORE = "seq_2"
F32 = jnp.float32
BF16 = jnp.bfloat16
T = 128
N = 128
PAIRS = 16
HEADS = 32
DOCS = 8
EXT = 8
Q = 4
HALF = PAIRS // 2
LOAD = 2 * N
PARTS = 4
PART = 512
FAR = -1e30
VMEM = pl.BlockSpec(memory_space=pltpu.VMEM)
SMEM = pl.BlockSpec(memory_space=pltpu.SMEM)
ANY = pl.BlockSpec(memory_space=pl.ANY)
HBM = pl.BlockSpec(memory_space=pltpu.HBM)

NN = (((1,), (0,)), ((), ()))
NT = (((1,), (1,)), ((), ()))
TN = (((0,), (0,)), ((), ()))


def dot(a, b, dims=NN, precision=None):
    return lax.dot_general(a, b, dims, precision=precision, preferred_element_type=F32)


def exact(a, b, dims=NN):
    return dot(a, b, dims, lax.Precision.HIGHEST)


def iota(shape, dim):
    return lax.broadcasted_iota(jnp.int32, shape, dim)


def block_base():
    return lax.axis_index(SEQ) * T


def doc_starts(len_ref):
    starts, at = [], jnp.int32(0)
    for d in range(DOCS):
        starts.append(at)
        at = at + len_ref[0, d]
    return starts


def segments(starts, base, offset):
    count = jnp.zeros(offset.shape, jnp.int32)
    for s in starts:
        local = jnp.where(s >= base, s - base, jnp.int32(1 << 20))
        count = count + (offset >= local).astype(jnp.int32)
    return count


def end_count(starts, base):
    count = jnp.int32(0)
    for s in starts:
        count = count + jnp.logical_and(s >= base, s < base + T).astype(jnp.int32)
    return count


def lower_triangle():
    return (iota((T, T), 1) <= iota((T, T), 0)).astype(F32)


def weights(ld, starts, base):
    log_cum = exact(lower_triangle(), ld, NT)
    seg = segments(starts, base, iota((T, HEADS), 0))
    last = end_count(starts, base)
    log_end = log_cum[T - 1 :, :]
    w_end = jnp.where(seg == last, jnp.exp(log_end - log_cum), 0.0)
    w_start = jnp.where(seg == 0, jnp.exp(log_cum), 0.0)
    gain = jnp.exp(log_end) * (last == 0).astype(F32)
    return w_end, w_start, gain


def spread(w, j, low):
    return jnp.where(low, w[:, 2 * j : 2 * j + 1], w[:, 2 * j + 1 : 2 * j + 2])


def cols(j):
    return slice(j * 128, (j + 1) * 128)


def heads_of(rows):
    lane = iota(rows.shape, 1)
    spot = lane & (HEADS - 1)
    row = iota(rows.shape, 0)
    even = jnp.sum(jnp.where(lane < 64, rows, 0.0), axis=1, keepdims=True)
    odd = jnp.sum(jnp.where(lane < 64, 0.0, rows), axis=1, keepdims=True)
    placed = jnp.where(spot == 2 * row, even, jnp.where(spot == 2 * row + 1, odd, 0.0))
    return jnp.sum(placed, axis=0, keepdims=True)


def is_first():
    return lax.axis_index(CORE) == 0


def shares(chunk):
    return [(q, i, HALF * chunk + 2 * q + i) for q in range(Q) for i in range(2)]


def rows_of(i):
    return slice(i * N, (i + 1) * N)


def local_sums(roles_ref, slot, j, w, low, p_t):
    own = roles_ref[slot, :, cols(j)].astype(F32)
    return dot(p_t, (own * spread(w, j, low)).astype(BF16))


def extra(gain_ref, chunk, q, skip):
    sub = iota((EXT, 128), 0)
    j = HALF * chunk + 2 * q
    block = jnp.where(sub == 0, gain_ref[j : j + 1], gain_ref[j + 1 : j + 2])
    return jnp.where(sub < 2, block, jnp.where(sub == 2, skip, 0.0))


def prep_kernel(
    len_hbm, v_hbm, g_hbm, b_hbm, c_hbm, ld_hbm,
    roles_ref, rows_ref, w_ref, gain_ref, send_ref,
    len_ref, ld_ref, small_sems, v_sems, g_sems,
):
    first = is_first()
    v_slot = jnp.where(first, 1, 0)
    g_slot = 1 - v_slot
    small = [
        pltpu.make_async_copy(len_hbm, len_ref, small_sems.at[0]),
        pltpu.make_async_copy(ld_hbm.at[0], ld_ref, small_sems.at[1]),
        pltpu.make_async_copy(b_hbm.at[0], rows_ref.at[v_slot], small_sems.at[2]),
        pltpu.make_async_copy(c_hbm.at[0], rows_ref.at[g_slot], small_sems.at[3]),
    ]
    for copy in small:
        copy.start()
    wide = []
    for k in range(PARTS):
        part = slice(k * PART, (k + 1) * PART)
        vc = pltpu.make_async_copy(
            v_hbm.at[0, :, part], roles_ref.at[v_slot, :, part], v_sems.at[k]
        )
        gc = pltpu.make_async_copy(
            g_hbm.at[0, :, part], roles_ref.at[g_slot, :, part], g_sems.at[k]
        )
        vc.start()
        gc.start()
        wide.append((vc, gc))
    for copy in small:
        copy.wait()
    starts = doc_starts(len_ref)
    w_end, w_start, gain = weights(ld_ref[...], starts, block_base())
    w = jnp.where(first, w_start, w_end)
    w_ref[0] = w
    w_ref[1] = jnp.where(first, w_end, w_start)
    p_t = rows_ref[0].T
    low = iota((T, 128), 1) < 64
    skips = []
    for j in range(PAIRS):
        if j % (PAIRS // PARTS) == 0:
            for copy in wide[j // (PAIRS // PARTS)]:
                copy.wait()
        gain_ref[j : j + 1] = spread(gain, j, low[:1])
        both = roles_ref[0, :, cols(j)].astype(F32) * roles_ref[1, :, cols(j)].astype(F32)
        skips.append(jnp.sum(both, axis=0, keepdims=True))
        if j < HALF:
            send_ref[j // 2, rows_of(j % 2)] = local_sums(roles_ref, 0, j, w, low, p_t)
    skip = heads_of(jnp.concatenate(skips, axis=0))
    for q in range(Q):
        send_ref[q, LOAD:] = extra(gain_ref, 0, q, skip)


def own_kernel(
    _, len_ref, skip_gain_ref, roles_ref, rows_ref, w_ref, mine_ref, keep_ref, gains_ref
):
    low = iota((T, 128), 1) < 64
    p_t = rows_ref[1].T
    w = w_ref[1]
    for q, i, j in shares(0):
        mine_ref[q, rows_of(i)] = local_sums(roles_ref, 1, j, w, low, p_t)
    for j in range(PAIRS):
        gains_ref[j : j + 1] = jnp.where(
            low[:1], skip_gain_ref[2 * j], skip_gain_ref[2 * j + 1]
        )
    base = block_base()
    starts = doc_starts(len_ref)
    offset = iota((EXT, T), 1)
    keep = jnp.ones((EXT, T), F32)
    for s in starts:
        keep = jnp.where(offset + base == s, 0.0, keep)
    keep_ref[...] = keep


def second_kernel(_, roles_ref, rows_ref, w_ref, gain_ref, send_ref, mine_ref):
    low = iota((T, 128), 1) < 64
    other_t = rows_ref[0].T
    mine_t = rows_ref[1].T
    w_other = w_ref[0]
    w_mine = w_ref[1]
    for q, i, j in shares(1):
        send_ref[q, rows_of(i)] = local_sums(roles_ref, 0, j, w_other, low, other_t)
        mine_ref[q, rows_of(i)] = local_sums(roles_ref, 1, j, w_mine, low, mine_t)
    for q in range(Q):
        send_ref[q, LOAD:] = extra(gain_ref, 1, q, 0.0)


def combine_kernel(recv_ref, mine_ref, send_ref, out_ref, buffer, sems):
    sub = iota((EXT, 128), 0)
    copies = []
    for q in range(Q):
        theirs = recv_ref[q, LOAD:]
        ours = send_ref[q, LOAD:]
        for i in range(2):
            r = rows_of(i)
            buffer[q, r] = theirs[i : i + 1] * mine_ref[q, r] + recv_ref[q, r]
        buffer[q, LOAD:] = jnp.where(sub == 2, theirs + ours, theirs * ours)
        copies.append(pltpu.make_async_copy(buffer.at[q], out_ref.at[q], sems.at[q]))
        copies[-1].start()
    for copy in copies:
        copy.wait()


def row_kernel(in_ref, prefix_ref, factor_ref, total_ref):
    first = is_first()
    sub = iota((EXT, 128), 0)
    place = iota((EXT, 128), 1) // HEADS == lax.axis_index(ROW)
    running = [jnp.zeros((N, 128), F32), jnp.zeros((N, 128), F32)]
    factor = jnp.ones((EXT, 128), F32)
    skip = jnp.zeros((EXT, 128), F32)
    for step in range(Q):
        at = jnp.where(first, step, Q - 1 - step)
        factor_ref[at] = factor
        ext = in_ref[at, LOAD:]
        for i in range(2):
            r = rows_of(i)
            prefix_ref[at, r] = running[i]
            running[i] = ext[i : i + 1] * running[i] + in_ref[at, r]
        factor = factor * ext
        skip = skip + in_ref[step, LOAD:]
    for i in range(2):
        total_ref[rows_of(i)] = running[i]
    total_ref[LOAD:] = jnp.where(sub == 2, jnp.where(place, skip, 0.0), factor)


def incoming(near_ref, next_ref, i):
    first = is_first()
    x = jnp.where(first, lax.axis_index(ROW), Q - 1 - lax.axis_index(ROW))
    r = rows_of(i)
    beyond = near_ref[LOAD + i : LOAD + i + 1] * next_ref[r]
    return jnp.where(x > 0, near_ref[r], 0.0) + jnp.where(x > 1, beyond, 0.0)


def enter(near_ref, next_ref, prefix_ref, factor_ref, buffer):
    for i in range(2):
        r = rows_of(i)
        start = incoming(near_ref, next_ref, i)
        for q in range(Q):
            buffer[q, r] = prefix_ref[q, r] + factor_ref[q, i : i + 1] * start


def send_out(buffer, out_ref, sems):
    copies = [pltpu.make_async_copy(buffer.at[q], out_ref.at[q], sems.at[q]) for q in range(Q)]
    for copy in copies:
        copy.start()
    for copy in copies:
        copy.wait()


def enter_first_kernel(
    near_ref, next_ref, prefix_ref, factor_ref, total_ref, skip_ref, out_ref, buffer, sems
):
    enter(near_ref, next_ref, prefix_ref, factor_ref, buffer)
    skip = jnp.where(is_first(), total_ref[LOAD:], next_ref[LOAD:]) + near_ref[LOAD:]
    skip_ref[...] = jnp.broadcast_to(skip[2:3], (EXT, 128))
    send_out(buffer, out_ref, sems)


def enter_second_kernel(
    near_ref, next_ref, prefix_ref, factor_ref, low_ref, high_ref, out_ref, buffer, sems
):
    enter(near_ref, next_ref, prefix_ref, factor_ref, buffer)
    plane = lax.axis_index("dp") + lax.axis_index(COL)
    sub = iota((EXT, 128), 0)
    ext = jnp.where(
        sub == (plane & 7),
        low_ref[...],
        jnp.where(sub == ((plane + 4) & 7), high_ref[...], 0.0),
    )
    for q in range(Q):
        buffer[q, LOAD:] = ext
    send_out(buffer, out_ref, sems)


def inside_kernel(_, len_ref, roles_ref, rows_ref, ld_ref, low_ref, high_ref, raw_ref):
    first = is_first()
    v_slot = jnp.where(first, 1, 0)
    g_slot = 1 - v_slot
    base = block_base()
    starts = doc_starts(len_ref)
    ld = ld_ref[0]
    tri = lower_triangle()
    cum_t = exact(tri, ld, NT)
    cum_h = exact(ld, tri, NT)
    t_at = iota((T, T), 0)
    s_at = iota((T, T), 1)
    same = segments(starts, base, t_at) == segments(starts, base, s_at)
    bias = jnp.where(jnp.logical_and(s_at <= t_at, same), 0.0, FAR)
    b = rows_ref[v_slot]
    c = rows_ref[g_slot]
    scores = dot(c, b, NT)
    low = iota((T, 128), 1) < 64
    zero = jnp.zeros((T, 128), BF16)
    grad_scores = jnp.zeros((T, T), F32)
    for j in range(PAIRS):
        v = roles_ref[v_slot, :, cols(j)]
        g = roles_ref[g_slot, :, cols(j)]
        v_two = jnp.concatenate([jnp.where(low, v, zero), jnp.where(low, zero, v)], axis=0)
        g_two = jnp.concatenate([jnp.where(low, g, zero), jnp.where(low, zero, g)], axis=0)
        grad_mix = dot(g, v_two, NT)
        mixes = []
        for k in range(2):
            h = 2 * j + k
            decay = jnp.exp(cum_t[:, h : h + 1] - cum_h[h : h + 1, :] + bias)
            mixes.append((scores * decay).astype(BF16))
            grad_scores = grad_scores + grad_mix[:, k * T : (k + 1) * T] * decay
        part_ref = low_ref if j < HALF else high_ref
        part_ref[g_slot, :, cols(j % HALF)] = dot(jnp.concatenate(mixes, axis=1), v_two)
        part_ref[v_slot, :, cols(j % HALF)] = dot(jnp.concatenate(mixes, axis=0), g_two, TN)
    half = grad_scores.astype(BF16)
    raw_ref[g_slot] = dot(half, b)
    raw_ref[v_slot] = dot(half, c, TN)


def pass_on_kernel(chunk, _, x_ref, mine_ref, gain_ref, out_ref):
    for q, i, j in shares(chunk):
        r = rows_of(i)
        out_ref[q, r] = gain_ref[j : j + 1] * x_ref[q, r] + mine_ref[q, r]
    if chunk == 1:
        skip = x_ref[0, LOAD:] + x_ref[1, LOAD:] + x_ref[2, LOAD:] + x_ref[3, LOAD:]
        for q in range(Q):
            out_ref[q, LOAD:] = skip


def finish_role(slot, chunk, j, low, x, roles_ref, rows, w, part_ref, skip_gains):
    half = x.astype(BF16)
    own = roles_ref[slot, :, cols(j)].astype(F32)
    skipped = roles_ref[1 - slot, :, cols(j)].astype(F32)
    wide = spread(w, j, low)
    tail = wide * dot(rows, half)
    out = part_ref[slot, :, cols(j - HALF * chunk)] + tail
    result = (out + skip_gains[j : j + 1] * skipped).astype(BF16)
    change = own * out
    hi = change.astype(BF16)
    lo = (change - hi.astype(F32)).astype(BF16)
    lane = iota((128, 128), 0)
    head = iota((128, 128), 1)
    pick = (head == 2 * j + jnp.where(lane < 64, 0, 1)).astype(BF16)
    end = jnp.sum(own * tail, axis=0, keepdims=True)
    return result, dot(hi, pick) + dot(lo, pick), end, dot((own * wide).astype(BF16), half, NT)


def finish_first_kernel(
    y_ref, x_ref, roles_ref, rows_ref, w_ref, part_ref, raw_ref, gains_ref, gain_ref,
    mixed_ref, vgrad_ref, total_ref, change_ref, end_ref,
):
    first = is_first()
    low = iota((T, 128), 1) < 64
    skip_gains = gains_ref[...]
    totals = [raw_ref[0], raw_ref[1]]
    changes = jnp.zeros((T, 128), F32)
    for q, i, j in shares(0):
        x = x_ref[q, rows_of(i)]
        y = y_ref[q, rows_of(i)]
        near, near_change, near_end, more = finish_role(
            0, 0, j, low, x, roles_ref, rows_ref[0], w_ref[0], part_ref, skip_gains
        )
        totals[0] = totals[0] + more
        far, far_change, far_end, more = finish_role(
            1, 0, j, low, y, roles_ref, rows_ref[1], w_ref[1], part_ref, skip_gains
        )
        totals[1] = totals[1] + more
        mixed_ref[:, cols(j)] = jnp.where(first, near, far)
        vgrad_ref[:, cols(j)] = jnp.where(first, far, near)
        changes = changes + near_change - far_change
        meet = jnp.sum(x * y, axis=0, keepdims=True)
        end_ref[j : j + 1] = jnp.where(first, far_end, near_end) + gain_ref[j : j + 1] * meet
    total_ref[0] = totals[0]
    total_ref[1] = totals[1]
    change_ref[...] = changes


def near_kernel(
    _, x_ref, roles_ref, rows_ref, w_ref, part_ref, gains_ref, total_in_ref, change_in_ref,
    out_ref, total_ref, change_ref, end_ref,
):
    low = iota((T, 128), 1) < 64
    skip_gains = gains_ref[...]
    total = total_in_ref[0]
    changes = change_in_ref[...]
    for q, i, j in shares(1):
        result, change, end, more = finish_role(
            0, 1, j, low, x_ref[q, rows_of(i)], roles_ref, rows_ref[0], w_ref[0], part_ref,
            skip_gains,
        )
        out_ref[:, cols(j - HALF)] = result
        changes = changes + change
        total = total + more
        end_ref[j - HALF : j - HALF + 1] = end
    total_ref[...] = total
    change_ref[...] = changes


def far_kernel(
    scales, y_ref, x_ref, passed_ref, roles_ref, rows_ref, w_ref, part_ref, gains_ref, gain_ref,
    keep_ref, mixed_in_ref, vgrad_in_ref, total_in_ref, end_in_ref,
    near_ref, near_total_ref, near_change_ref, near_end_ref,
    igrad_ref, ograd_ref, dgrad_ref, skip_ref, mixed_hbm, vgrad_hbm,
    mixed_ref, vgrad_ref, sems,
):
    in_scale, out_scale, decay_scale, skip_scale = scales
    first = is_first()
    low = iota((T, 128), 1) < 64
    skip_gains = gains_ref[...]
    copies = []

    def leave(src, dst, lo, hi, sem):
        copies.append(pltpu.make_async_copy(src, dst.at[0, :, lo:hi], sem))
        copies[-1].start()

    middle = HALF * 128
    leave(mixed_in_ref, mixed_hbm, 0, middle, sems.at[0, 0])
    leave(vgrad_in_ref, vgrad_hbm, 0, middle, sems.at[1, 0])
    total = total_in_ref[1]
    changes = near_change_ref[...]
    ends = [end_in_ref[...]]
    for q, i, j in shares(1):
        y = y_ref[q, rows_of(i)]
        result, change, end, more = finish_role(
            1, 1, j, low, y, roles_ref, rows_ref[1], w_ref[1], part_ref, skip_gains
        )
        k = j - HALF
        near = near_ref[:, cols(k)]
        mixed_ref[:, cols(k)] = jnp.where(first, near, result)
        vgrad_ref[:, cols(k)] = jnp.where(first, result, near)
        if k % 4 == 3:
            part = slice((k - 3) * 128, (k + 1) * 128)
            lo, hi = middle + part.start, middle + part.stop
            leave(mixed_ref.at[:, part], mixed_hbm, lo, hi, sems.at[0, 1 + k // 4])
            leave(vgrad_ref.at[:, part], vgrad_hbm, lo, hi, sems.at[1, 1 + k // 4])
        changes = changes - change
        total = total + more
        meet = jnp.sum(x_ref[q, rows_of(i)] * y, axis=0, keepdims=True)
        end = jnp.where(first, end, near_end_ref[k : k + 1])
        ends.append(end + gain_ref[j : j + 1] * meet)
    near_total = near_total_ref[...]
    igrad_ref[0] = jnp.where(first, total, near_total) * in_scale
    ograd_ref[0] = jnp.where(first, near_total, total) * out_scale
    changes = jnp.where(first, changes, -changes)
    at_end = iota((T, 128), 0) == T - 1
    changes = changes + jnp.where(at_end, heads_of(jnp.concatenate(ends, axis=0)), 0.0)
    summed = exact(changes, lower_triangle(), TN)[:HEADS]
    dgrad_ref[0] = summed * keep_ref[:1] * decay_scale
    skips = jnp.sum(passed_ref[0, LOAD:] + y_ref[0, LOAD:], axis=0, keepdims=True)
    skip = skips[:, :HEADS]
    for x in range(1, Q):
        skip = skip + skips[:, x * HEADS : (x + 1) * HEADS]
    skip_ref[...] = skip * skip_scale
    for copy in copies:
        copy.wait()


def call(kernel, outs, *args, after=(), spaces=(), out_spaces=(), scratch=(), flops=0, moved=0):
    in_specs = [ANY] * len(after) + list(spaces)
    in_specs += [VMEM] * (len(args) + len(after) - len(in_specs))
    out_specs = [VMEM] * (len(outs) - len(out_spaces)) + list(out_spaces)
    return pl.pallas_call(
        kernel,
        out_shape=tuple(outs),
        in_specs=in_specs,
        out_specs=tuple(out_specs),
        scratch_shapes=list(scratch),
        compiler_params=pltpu.CompilerParams(vmem_limit_bytes=16 << 20),
        cost_estimate=pl.CostEstimate(flops=flops, bytes_accessed=moved, transcendentals=0),
    )(*after, *args)


def f32(*shape):
    return jax.ShapeDtypeStruct(shape, F32)


def bf16(*shape):
    return jax.ShapeDtypeStruct(shape, BF16)


def dma(*shape):
    return pltpu.SemaphoreType.DMA(shape)


def swap_cores(x):
    return lax.ppermute(x, CORE, [(0, 1), (1, 0)])


def along_row(x):
    return lax.all_to_all(x, COL, split_axis=0, concat_axis=0, tiled=True)


def to_row(x, step):
    pairs = []
    for r in range(Q):
        pairs.append((2 * r, 2 * ((r + step) % Q)))
        pairs.append((2 * r + 1, 2 * ((r - step) % Q) + 1))
    return lax.ppermute(x, (ROW, CORE), pairs)


def from_plane(x, offset):
    pairs = []
    for d in range(8):
        for y in range(Q):
            pairs.append((((d + y + offset) % 8) * Q + y, d * Q + y))
    return lax.ppermute(x, ("dp", COL), pairs)


def body(values_in, input_proj, output_proj, log_decay, doc_lengths, skip_gain, out_cotangent):
    inputs = (doc_lengths, values_in, out_cotangent, input_proj, output_proj, log_decay)
    token_count = lax.axis_size(SEQ) * T
    seq_count = lax.axis_size("dp")
    inner = values_in.shape[2]
    head_dim = inner // HEADS
    loaded = f32(Q, LOAD + EXT, 128)
    plain = f32(Q, LOAD, 128)

    def leaving(shape):
        return dict(
            out_spaces=[HBM], scratch=[pltpu.VMEM(shape.shape, F32), dma(Q)], moved=2 << 20
        )

    roles, rows, w, gain, send_a = call(
        prep_kernel,
        (bf16(2, T, inner), bf16(2, T, N), f32(2, T, HEADS), f32(PAIRS, 128), loaded),
        *(pltpu.with_memory_space_constraint(a, pltpu.HBM) for a in inputs),
        spaces=[HBM] * 6,
        scratch=[
            pltpu.SMEM((1, DOCS), jnp.int32), pltpu.VMEM((HEADS, T), F32),
            dma(4), dma(PARTS), dma(PARTS),
        ],
        moved=4 << 20,
    )
    recv_a = swap_cores(send_a)
    mine_a, keep, gains = call(
        own_kernel,
        (plain, f32(EXT, T), f32(PAIRS, 128)),
        doc_lengths, skip_gain, roles, rows, w,
        after=(send_a,),
        spaces=[SMEM] * 2,
        moved=4 << 20,
    )
    (chip_a,) = call(combine_kernel, (loaded,), recv_a, mine_a, send_a, **leaving(loaded))
    in_a = along_row(chip_a)
    send_b, mine_b = call(
        second_kernel, (loaded, plain), roles, rows, w, gain, after=(chip_a,), moved=4 << 20
    )
    recv_b = swap_cores(send_b)
    (chip_b,) = call(combine_kernel, (loaded,), recv_b, mine_b, send_b, **leaving(loaded))
    scanned = (plain, f32(Q, EXT, 128), f32(LOAD + EXT, 128))
    prefix_a, factor_a, total_a = call(row_kernel, scanned, in_a, moved=1 << 20)
    in_b = along_row(chip_b)
    skip, out_a = call(
        enter_first_kernel,
        (f32(EXT, 128), plain),
        to_row(total_a, 1), to_row(total_a, 2), prefix_a, factor_a, total_a,
        **leaving(plain),
    )
    prefix_b, factor_b, total_b = call(row_kernel, scanned, in_b, moved=1 << 20)
    x_a = along_row(out_a)
    (out_b,) = call(
        enter_second_kernel,
        (loaded,),
        to_row(total_b, 1), to_row(total_b, 2), prefix_b, factor_b,
        from_plane(skip, 0), from_plane(skip, 4),
        **leaving(loaded),
    )
    (passed_a,) = call(
        functools.partial(pass_on_kernel, 0), (plain,), x_a, mine_a, gain, after=(out_b,),
        moved=1 << 20,
    )
    x_b = along_row(out_b)
    y_a = swap_cores(passed_a)
    part_a, part_b, raw = call(
        inside_kernel,
        (f32(2, T, inner // 2), f32(2, T, inner // 2), f32(2, T, N)),
        doc_lengths, roles, rows, log_decay,
        after=(out_b,),
        spaces=[SMEM],
        flops=40 * 2 * T * N * inner,
        moved=20 << 20,
    )
    mixed_a, vgrad_a, total, change, end = call(
        finish_first_kernel,
        (bf16(T, inner // 2), bf16(T, inner // 2), f32(2, T, N), f32(T, 128), f32(HALF, 128)),
        y_a, x_a, roles, rows, w, part_a, raw, gains, gain,
        moved=8 << 20,
    )
    (passed_b,) = call(
        functools.partial(pass_on_kernel, 1), (loaded,), x_b, mine_b, gain, after=(change,),
        moved=1 << 20,
    )
    y_b = swap_cores(passed_b)
    near = call(
        near_kernel,
        (bf16(T, inner // 2), f32(T, N), f32(T, 128), f32(HALF, 128)),
        x_b, roles, rows, w, part_b, gains, total, change,
        after=(passed_b,),
        moved=4 << 20,
    )
    scales = (
        1.0 / inner**0.5,
        (N / (inner * token_count)) ** 0.5,
        1.0 / (head_dim * token_count) ** 0.5,
        1.0 / (seq_count * token_count * head_dim) ** 0.5,
    )
    input_grad, output_grad, decay_grad, skip_grad, mixed, values_grad = call(
        functools.partial(far_kernel, scales),
        (
            f32(1, T, N), f32(1, T, N), f32(1, HEADS, T), f32(1, HEADS),
            bf16(1, T, inner), bf16(1, T, inner),
        ),
        y_b, x_b, passed_b, roles, rows, w, part_b, gains, gain, keep,
        mixed_a, vgrad_a, total, end, *near,
        out_spaces=[HBM] * 2,
        scratch=[
            pltpu.VMEM((T, inner // 2), BF16), pltpu.VMEM((T, inner // 2), BF16), dma(2, 3)
        ],
        moved=8 << 20,
    )
    return mixed, values_grad, input_grad, output_grad, decay_grad, skip_grad[0]


def solution(mesh):
    finer = Mesh(mesh.devices.reshape(mesh.shape["dp"], 4, 4, 2), ("dp",) + SEQ)
    placed = (
        P("dp", SEQ, None),
        P("dp", SEQ, None),
        P("dp", SEQ, None),
        P("dp", None, SEQ),
        P("dp", None),
        P(),
        P("dp", SEQ, None),
    )
    return jax.shard_map(
        body,
        mesh=finer,
        in_specs=placed,
        out_specs=(
            P("dp", SEQ, None),
            P("dp", SEQ, None),
            P("dp", SEQ, None),
            P("dp", SEQ, None),
            P("dp", None, SEQ),
            P(),
        ),
        check_vma=False,
    )
```

```python
import functools

import jax
import jax.numpy as jnp
from jax import lax
from jax.experimental import pallas as pl
from jax.experimental.pallas import tpu as pltpu
from jax.sharding import Mesh
from jax.sharding import PartitionSpec as P


SEQ = ("seq_0", "seq_1", "seq_2")
ROW, COL = "seq_0", "seq_1"
CORE = "seq_2"
F32 = jnp.float32
BF16 = jnp.bfloat16
T = 128
N = 128
PAIRS = 16
HEADS = 32
DOCS = 8
EXT = 8
Q = 4
DEEP = PAIRS // Q
LOAD = DEEP * N
SKIP = DEEP
PARTS = 4
PART = 512
FAR = -1e30
VMEM = pl.BlockSpec(memory_space=pltpu.VMEM)
SMEM = pl.BlockSpec(memory_space=pltpu.SMEM)
ANY = pl.BlockSpec(memory_space=pl.ANY)
HBM = pl.BlockSpec(memory_space=pltpu.HBM)

NN = (((1,), (0,)), ((), ()))
NT = (((1,), (1,)), ((), ()))
TN = (((0,), (0,)), ((), ()))


def dot(a, b, dims=NN, precision=None):
    return lax.dot_general(a, b, dims, precision=precision, preferred_element_type=F32)


def exact(a, b, dims=NN):
    return dot(a, b, dims, lax.Precision.HIGHEST)


def iota(shape, dim):
    return lax.broadcasted_iota(jnp.int32, shape, dim)


def block_base():
    return lax.axis_index(SEQ) * T


def doc_starts(len_ref):
    starts, at = [], jnp.int32(0)
    for d in range(DOCS):
        starts.append(at)
        at = at + len_ref[0, d]
    return starts


def segments(starts, base, offset):
    count = jnp.zeros(offset.shape, jnp.int32)
    for s in starts:
        local = jnp.where(s >= base, s - base, jnp.int32(1 << 20))
        count = count + (offset >= local).astype(jnp.int32)
    return count


def end_count(starts, base):
    count = jnp.int32(0)
    for s in starts:
        count = count + jnp.logical_and(s >= base, s < base + T).astype(jnp.int32)
    return count


def lower_triangle():
    return (iota((T, T), 1) <= iota((T, T), 0)).astype(F32)


def weights(ld, starts, base):
    log_cum = exact(lower_triangle(), ld, NT)
    seg = segments(starts, base, iota((T, HEADS), 0))
    last = end_count(starts, base)
    log_end = log_cum[T - 1 :, :]
    w_end = jnp.where(seg == last, jnp.exp(log_end - log_cum), 0.0)
    w_start = jnp.where(seg == 0, jnp.exp(log_cum), 0.0)
    gain = jnp.exp(log_end) * (last == 0).astype(F32)
    return w_end, w_start, gain


def spread(w, j, low):
    return jnp.where(low, w[:, 2 * j : 2 * j + 1], w[:, 2 * j + 1 : 2 * j + 2])


def cols(j):
    return slice(j * 128, (j + 1) * 128)


def heads_of(rows):
    lane = iota(rows.shape, 1)
    spot = lane & (HEADS - 1)
    row = iota(rows.shape, 0)
    even = jnp.sum(jnp.where(lane < 64, rows, 0.0), axis=1, keepdims=True)
    odd = jnp.sum(jnp.where(lane < 64, 0.0, rows), axis=1, keepdims=True)
    placed = jnp.where(spot == 2 * row, even, jnp.where(spot == 2 * row + 1, odd, 0.0))
    return jnp.sum(placed, axis=0, keepdims=True)


def is_first():
    return lax.axis_index(CORE) == 0


def pairs_of(q):
    return [(i, DEEP * q + i) for i in range(DEEP)]


def rows_of(i):
    return slice(i * N, (i + 1) * N)


def local_sums(roles_ref, slot, j, w, low, p_t):
    own = roles_ref[slot, :, cols(j)].astype(F32)
    return dot(p_t, (own * spread(w, j, low)).astype(BF16))


def prep_kernel(
    len_hbm, v_hbm, g_hbm, b_hbm, c_hbm, ld_hbm,
    roles_ref, rows_ref, w_ref, gain_ref, send_ref,
    len_ref, ld_ref, small_sems, v_sems, g_sems,
):
    first = is_first()
    v_slot = jnp.where(first, 1, 0)
    g_slot = 1 - v_slot
    small = [
        pltpu.make_async_copy(len_hbm, len_ref, small_sems.at[0]),
        pltpu.make_async_copy(ld_hbm.at[0], ld_ref, small_sems.at[1]),
        pltpu.make_async_copy(b_hbm.at[0], rows_ref.at[v_slot], small_sems.at[2]),
        pltpu.make_async_copy(c_hbm.at[0], rows_ref.at[g_slot], small_sems.at[3]),
    ]
    for copy in small:
        copy.start()
    wide = []
    for k in range(PARTS):
        part = slice(k * PART, (k + 1) * PART)
        vc = pltpu.make_async_copy(
            v_hbm.at[0, :, part], roles_ref.at[v_slot, :, part], v_sems.at[k]
        )
        gc = pltpu.make_async_copy(
            g_hbm.at[0, :, part], roles_ref.at[g_slot, :, part], g_sems.at[k]
        )
        vc.start()
        gc.start()
        wide.append((vc, gc))
    for copy in small:
        copy.wait()
    starts = doc_starts(len_ref)
    w_end, w_start, gain = weights(ld_ref[...], starts, block_base())
    w = jnp.where(first, w_start, w_end)
    w_ref[0] = w
    w_ref[1] = jnp.where(first, w_end, w_start)
    p_t = rows_ref[0].T
    low = iota((T, 128), 1) < 64
    skips = []
    for j in range(PAIRS):
        if j % (PAIRS // PARTS) == 0:
            for copy in wide[j // (PAIRS // PARTS)]:
                copy.wait()
        gain_ref[j : j + 1] = spread(gain, j, low[:1])
        both = roles_ref[0, :, cols(j)].astype(F32) * roles_ref[1, :, cols(j)].astype(F32)
        skips.append(jnp.sum(both, axis=0, keepdims=True))
        send_ref[j // DEEP, rows_of(j % DEEP)] = local_sums(roles_ref, 0, j, w, low, p_t)
    skip = heads_of(jnp.concatenate(skips, axis=0))
    sub = iota((EXT, 128), 0)
    for q in range(Q):
        ext = jnp.where(sub == SKIP, skip, 0.0)
        for i, j in pairs_of(q):
            ext = jnp.where(sub == i, gain_ref[j : j + 1], ext)
        send_ref[q, LOAD:] = ext


def own_kernel(
    _, len_ref, skip_gain_ref, roles_ref, rows_ref, w_ref, mine_ref, keep_ref, gains_ref
):
    low = iota((T, 128), 1) < 64
    p_t = rows_ref[1].T
    w = w_ref[1]
    for j in range(PAIRS):
        mine_ref[j // DEEP, rows_of(j % DEEP)] = local_sums(roles_ref, 1, j, w, low, p_t)
        gains_ref[j : j + 1] = jnp.where(
            low[:1], skip_gain_ref[2 * j], skip_gain_ref[2 * j + 1]
        )
    base = block_base()
    starts = doc_starts(len_ref)
    offset = iota((EXT, T), 1)
    keep = jnp.ones((EXT, T), F32)
    for s in starts:
        keep = jnp.where(offset + base == s, 0.0, keep)
    keep_ref[...] = keep


def column(shift):
    return (lax.axis_index(COL) + shift) & (Q - 1)


def combine_kernel(recv_ref, mine_ref, send_ref, *out_refs):
    sub = iota((EXT, 128), 0)
    for step, out_ref in enumerate(out_refs):
        q = column(step)
        theirs = recv_ref[q, LOAD:]
        ours = send_ref[q, LOAD:]
        for i in range(DEEP):
            r = rows_of(i)
            out_ref[r] = theirs[i : i + 1] * mine_ref[q, r] + recv_ref[q, r]
        out_ref[LOAD:] = jnp.where(sub == SKIP, theirs + ours, theirs * ours)


def row_kernel(_, a_ref, b_ref, c_ref, d_ref, prefix_ref, factor_ref, total_ref, in_ref):
    first = is_first()
    sub = iota((EXT, 128), 0)
    place = iota((EXT, 128), 1) // HEADS == lax.axis_index(ROW)
    for step, ref in enumerate((a_ref, b_ref, c_ref, d_ref)):
        in_ref[column(-step)] = ref[...]
    running = [jnp.zeros((N, 128), F32)] * DEEP
    factor = jnp.ones((EXT, 128), F32)
    skip = jnp.zeros((EXT, 128), F32)
    for step in range(Q):
        at = jnp.where(first, step, Q - 1 - step)
        factor_ref[at] = factor
        ext = in_ref[at, LOAD:]
        for i in range(DEEP):
            r = rows_of(i)
            prefix_ref[at, r] = running[i]
            running[i] = ext[i : i + 1] * running[i] + in_ref[at, r]
        factor = factor * ext
        skip = skip + in_ref[step, LOAD:]
    for i in range(DEEP):
        total_ref[rows_of(i)] = running[i]
    total_ref[LOAD:] = jnp.where(sub == SKIP, jnp.where(place, skip, 0.0), factor)


def enter_kernel(near_ref, next_ref, prefix_ref, factor_ref, total_ref, skip_ref, *out_refs):
    first = is_first()
    x = jnp.where(first, lax.axis_index(ROW), Q - 1 - lax.axis_index(ROW))
    skip = jnp.where(first, total_ref[LOAD:], next_ref[LOAD:]) + near_ref[LOAD:]
    skip_ref[...] = jnp.broadcast_to(skip[SKIP : SKIP + 1], (EXT, 128))
    for i in range(DEEP):
        r = rows_of(i)
        beyond = near_ref[LOAD + i : LOAD + i + 1] * next_ref[r]
        start = jnp.where(x > 0, near_ref[r], 0.0) + jnp.where(x > 1, beyond, 0.0)
        for step, out_ref in enumerate(out_refs):
            q = column(step)
            out_ref[r] = prefix_ref[q, r] + factor_ref[q, i : i + 1] * start


def planes_kernel(low_ref, high_ref, out_ref):
    plane = lax.axis_index("dp") + lax.axis_index(COL)
    sub = iota((EXT, 128), 0)
    high = jnp.where(sub == ((plane + 4) & 7), high_ref[...], 0.0)
    out_ref[...] = jnp.where(sub == (plane & 7), low_ref[...], high)


def inside_kernel(_, len_ref, roles_ref, rows_ref, ld_ref, part_ref, raw_ref):
    first = is_first()
    v_slot = jnp.where(first, 1, 0)
    g_slot = 1 - v_slot
    base = block_base()
    starts = doc_starts(len_ref)
    ld = ld_ref[0]
    tri = lower_triangle()
    cum_t = exact(tri, ld, NT)
    cum_h = exact(ld, tri, NT)
    t_at = iota((T, T), 0)
    s_at = iota((T, T), 1)
    same = segments(starts, base, t_at) == segments(starts, base, s_at)
    bias = jnp.where(jnp.logical_and(s_at <= t_at, same), 0.0, FAR)
    b = rows_ref[v_slot]
    c = rows_ref[g_slot]
    scores = dot(c, b, NT)
    low = iota((T, 128), 1) < 64
    zero = jnp.zeros((T, 128), BF16)
    grad_scores = jnp.zeros((T, T), F32)
    for j in range(PAIRS):
        v = roles_ref[v_slot, :, cols(j)]
        g = roles_ref[g_slot, :, cols(j)]
        v_two = jnp.concatenate([jnp.where(low, v, zero), jnp.where(low, zero, v)], axis=0)
        g_two = jnp.concatenate([jnp.where(low, g, zero), jnp.where(low, zero, g)], axis=0)
        grad_mix = dot(g, v_two, NT)
        mixes = []
        for k in range(2):
            h = 2 * j + k
            decay = jnp.exp(cum_t[:, h : h + 1] - cum_h[h : h + 1, :] + bias)
            mixes.append((scores * decay).astype(BF16))
            grad_scores = grad_scores + grad_mix[:, k * T : (k + 1) * T] * decay
        part_ref[g_slot, :, cols(j)] = dot(jnp.concatenate(mixes, axis=1), v_two)
        part_ref[v_slot, :, cols(j)] = dot(jnp.concatenate(mixes, axis=0), g_two, TN)
    half = grad_scores.astype(BF16)
    raw_ref[g_slot] = dot(half, b)
    raw_ref[v_slot] = dot(half, c, TN)


def pass_on_kernel(
    a_ref, b_ref, c_ref, d_ref, z0_ref, z1_ref, z2_ref, z3_ref, mine_ref, gain_ref,
    out_ref, x_ref,
):
    for step, ref in enumerate((a_ref, b_ref, c_ref, d_ref)):
        x_ref[column(-step)] = ref[...]
    for q in range(Q):
        for i, j in pairs_of(q):
            r = rows_of(i)
            out_ref[q, r] = gain_ref[j : j + 1] * x_ref[q, r] + mine_ref[q, r]
        out_ref[q, LOAD:] = z0_ref[...] + z1_ref[...] + z2_ref[...] + z3_ref[...]


def finish_role(slot, j, low, x, roles_ref, rows, w, part_ref, skip_gains):
    half = x.astype(BF16)
    own = roles_ref[slot, :, cols(j)].astype(F32)
    skipped = roles_ref[1 - slot, :, cols(j)].astype(F32)
    wide = spread(w, j, low)
    tail = wide * dot(rows, half)
    out = part_ref[slot, :, cols(j)] + tail
    result = (out + skip_gains[j : j + 1] * skipped).astype(BF16)
    change = own * out
    hi = change.astype(BF16)
    lo = (change - hi.astype(F32)).astype(BF16)
    lane = iota((128, 128), 0)
    head = iota((128, 128), 1)
    pick = (head == 2 * j + jnp.where(lane < 64, 0, 1)).astype(BF16)
    end = jnp.sum(own * tail, axis=0, keepdims=True)
    return result, dot(hi, pick) + dot(lo, pick), end, dot((own * wide).astype(BF16), half, NT)


def near_kernel(
    _, x_ref, roles_ref, rows_ref, w_ref, part_ref, raw_ref, gains_ref,
    out_ref, total_ref, change_ref, end_ref,
):
    low = iota((T, 128), 1) < 64
    rows = rows_ref[0]
    w = w_ref[0]
    skip_gains = gains_ref[...]
    total = raw_ref[0]
    changes = jnp.zeros((T, 128), F32)
    for j in range(PAIRS):
        x = x_ref[j // DEEP, rows_of(j % DEEP)]
        result, change, end, more = finish_role(
            0, j, low, x, roles_ref, rows, w, part_ref, skip_gains
        )
        out_ref[:, cols(j)] = result
        changes = changes + change
        total = total + more
        end_ref[j : j + 1] = end
    total_ref[...] = total
    change_ref[...] = changes


def far_kernel(
    scales, y_ref, x_ref, passed_ref, roles_ref, rows_ref, w_ref, part_ref, raw_ref, gains_ref,
    gain_ref, keep_ref, near_ref, near_total_ref, near_change_ref, near_end_ref,
    igrad_ref, ograd_ref, dgrad_ref, skip_ref, mixed_hbm, vgrad_hbm,
    mixed_ref, vgrad_ref, sems,
):
    in_scale, out_scale, decay_scale, skip_scale = scales
    first = is_first()
    low = iota((T, 128), 1) < 64
    rows = rows_ref[1]
    w = w_ref[1]
    skip_gains = gains_ref[...]
    total = raw_ref[1]
    changes = near_change_ref[...]
    ends = []
    copies = []
    for j in range(PAIRS):
        q, r = j // DEEP, rows_of(j % DEEP)
        y = y_ref[q, r]
        result, change, end, more = finish_role(
            1, j, low, y, roles_ref, rows, w, part_ref, skip_gains
        )
        near = near_ref[:, cols(j)]
        mixed_ref[:, cols(j)] = jnp.where(first, near, result)
        vgrad_ref[:, cols(j)] = jnp.where(first, result, near)
        if (j + 1) % (PAIRS // PARTS) == 0:
            k = j // (PAIRS // PARTS)
            part = slice(k * PART, (k + 1) * PART)
            for n, (src, dst) in enumerate(((mixed_ref, mixed_hbm), (vgrad_ref, vgrad_hbm))):
                copies.append(
                    pltpu.make_async_copy(src.at[:, part], dst.at[0, :, part], sems.at[n, k])
                )
                copies[-1].start()
        changes = changes - change
        total = total + more
        meet = jnp.sum(x_ref[q, r] * y, axis=0, keepdims=True)
        end = jnp.where(first, end, near_end_ref[j : j + 1])
        ends.append(end + gain_ref[j : j + 1] * meet)
    near_total = near_total_ref[...]
    igrad_ref[0] = jnp.where(first, total, near_total) * in_scale
    ograd_ref[0] = jnp.where(first, near_total, total) * out_scale
    changes = jnp.where(first, changes, -changes)
    at_end = iota((T, 128), 0) == T - 1
    changes = changes + jnp.where(at_end, heads_of(jnp.concatenate(ends, axis=0)), 0.0)
    summed = exact(changes, lower_triangle(), TN)[:HEADS]
    dgrad_ref[0] = summed * keep_ref[:1] * decay_scale
    skips = jnp.sum(passed_ref[0, LOAD:] + y_ref[0, LOAD:], axis=0, keepdims=True)
    skip = skips[:, :HEADS]
    for x in range(1, Q):
        skip = skip + skips[:, x * HEADS : (x + 1) * HEADS]
    skip_ref[...] = skip * skip_scale
    for copy in copies:
        copy.wait()


def call(kernel, outs, *args, after=(), spaces=(), out_spaces=(), scratch=(), flops=0, moved=0):
    in_specs = [ANY] * len(after) + list(spaces)
    in_specs += [VMEM] * (len(args) + len(after) - len(in_specs))
    out_specs = [VMEM] * (len(outs) - len(out_spaces)) + list(out_spaces)
    return pl.pallas_call(
        kernel,
        out_shape=tuple(outs),
        in_specs=in_specs,
        out_specs=tuple(out_specs),
        scratch_shapes=list(scratch),
        compiler_params=pltpu.CompilerParams(vmem_limit_bytes=16 << 20),
        cost_estimate=pl.CostEstimate(flops=flops, bytes_accessed=moved, transcendentals=0),
    )(*after, *args)


def f32(*shape):
    return jax.ShapeDtypeStruct(shape, F32)


def bf16(*shape):
    return jax.ShapeDtypeStruct(shape, BF16)


def dma(*shape):
    return pltpu.SemaphoreType.DMA(shape)


def swap_cores(x):
    return lax.ppermute(x, CORE, [(0, 1), (1, 0)])


def along_row(x, step):
    return lax.ppermute(x, COL, [(y, (y + step) % Q) for y in range(Q)])


def to_row(x, step):
    pairs = []
    for r in range(Q):
        pairs.append((2 * r, 2 * ((r + step) % Q)))
        pairs.append((2 * r + 1, 2 * ((r - step) % Q) + 1))
    return lax.ppermute(x, (ROW, CORE), pairs)


def from_plane(x, offset):
    pairs = []
    for d in range(8):
        for y in range(Q):
            pairs.append((((d + y + offset) % 8) * Q + y, d * Q + y))
    return lax.ppermute(x, ("dp", COL), pairs)


def body(values_in, input_proj, output_proj, log_decay, doc_lengths, skip_gain, out_cotangent):
    inputs = (doc_lengths, values_in, out_cotangent, input_proj, output_proj, log_decay)
    token_count = lax.axis_size(SEQ) * T
    seq_count = lax.axis_size("dp")
    inner = values_in.shape[2]
    head_dim = inner // HEADS
    loaded = f32(Q, LOAD + EXT, 128)
    plain = f32(Q, LOAD, 128)
    share = f32(LOAD + EXT, 128)
    small = f32(EXT, 128)
    roles, rows, w, gain, send = call(
        prep_kernel,
        (bf16(2, T, inner), bf16(2, T, N), f32(2, T, HEADS), f32(PAIRS, 128), loaded),
        *(pltpu.with_memory_space_constraint(a, pltpu.HBM) for a in inputs),
        spaces=[HBM] * 6,
        scratch=[
            pltpu.SMEM((1, DOCS), jnp.int32), pltpu.VMEM((HEADS, T), F32),
            dma(4), dma(PARTS), dma(PARTS),
        ],
        moved=4 << 20,
    )
    recv = swap_cores(send)
    mine, keep, gains = call(
        own_kernel,
        (plain, small, f32(PAIRS, 128)),
        doc_lengths, skip_gain, roles, rows, w,
        after=(send,),
        spaces=[SMEM] * 2,
        moved=4 << 20,
    )
    chip = call(combine_kernel, (share,) * Q, recv, mine, send, moved=3 << 20)
    arrived = [along_row(chip[step], step) for step in range(1, Q)]
    part, raw = call(
        inside_kernel,
        (f32(2, T, inner), f32(2, T, N)),
        doc_lengths, roles, rows, log_decay,
        after=(chip[0],),
        spaces=[SMEM],
        moved=12 << 20,
    )
    prefix, factor, total = call(
        row_kernel,
        (plain, f32(Q, EXT, 128), share),
        chip[0], *arrived,
        after=(raw,),
        scratch=[pltpu.VMEM((Q, LOAD + EXT, 128), F32)],
        moved=2 << 20,
    )
    skip, *entered = call(
        enter_kernel,
        (small,) + (f32(LOAD, 128),) * Q,
        to_row(total, 1), to_row(total, 2), prefix, factor, total,
        moved=2 << 20,
    )
    returned = [along_row(entered[step], step) for step in range(1, Q)]
    (planes,) = call(
        planes_kernel, (small,), from_plane(skip, 0), from_plane(skip, 4), moved=1 << 14
    )
    passed, x = call(
        pass_on_kernel,
        (loaded, plain),
        entered[0], *returned,
        planes, *(along_row(planes, step) for step in range(1, Q)),
        mine, gain,
        moved=3 << 20,
    )
    y = swap_cores(passed)
    near = call(
        near_kernel,
        (bf16(T, inner), f32(T, N), f32(T, 128), f32(PAIRS, 128)),
        x, roles, rows, w, part, raw, gains,
        after=(passed,),
        moved=8 << 20,
    )
    scales = (
        1.0 / inner**0.5,
        (N / (inner * token_count)) ** 0.5,
        1.0 / (head_dim * token_count) ** 0.5,
        1.0 / (seq_count * token_count * head_dim) ** 0.5,
    )
    input_grad, output_grad, decay_grad, skip_grad, mixed, values_grad = call(
        functools.partial(far_kernel, scales),
        (
            f32(1, T, N), f32(1, T, N), f32(1, HEADS, T), f32(1, HEADS),
            bf16(1, T, inner), bf16(1, T, inner),
        ),
        y, x, passed, roles, rows, w, part, raw, gains, gain, keep, *near,
        out_spaces=[HBM] * 2,
        scratch=[pltpu.VMEM((T, inner), BF16), pltpu.VMEM((T, inner), BF16), dma(2, PARTS)],
        moved=8 << 20,
    )
    return mixed, values_grad, input_grad, output_grad, decay_grad, skip_grad[0]


def solution(mesh):
    finer = Mesh(mesh.devices.reshape(mesh.shape["dp"], 4, 4, 2), ("dp",) + SEQ)
    placed = (
        P("dp", SEQ, None),
        P("dp", SEQ, None),
        P("dp", SEQ, None),
        P("dp", None, SEQ),
        P("dp", None),
        P(),
        P("dp", SEQ, None),
    )
    return jax.shard_map(
        body,
        mesh=finer,
        in_specs=placed,
        out_specs=(
            P("dp", SEQ, None),
            P("dp", SEQ, None),
            P("dp", SEQ, None),
            P("dp", SEQ, None),
            P("dp", None, SEQ),
            P(),
        ),
        check_vma=False,
    )
```

```python
import functools

import jax
import jax.numpy as jnp
from jax import lax
from jax.experimental import pallas as pl
from jax.experimental.pallas import tpu as pltpu
from jax.sharding import Mesh
from jax.sharding import PartitionSpec as P


SEQ = ("seq_0", "seq_1", "seq_2")
CHIPS = ("seq_0", "seq_1")
CORE = "seq_2"
F32 = jnp.float32
BF16 = jnp.bfloat16
T = 128
N = 128
PAIRS = 16
HEADS = 32
DOCS = 8
EXT = 8
PARTS = 4
PART = 512
FAR = -1e30
VMEM = pl.BlockSpec(memory_space=pltpu.VMEM)
SMEM = pl.BlockSpec(memory_space=pltpu.SMEM)
ANY = pl.BlockSpec(memory_space=pl.ANY)
HBM = pl.BlockSpec(memory_space=pltpu.HBM)

NN = (((1,), (0,)), ((), ()))
NT = (((1,), (1,)), ((), ()))
TN = (((0,), (0,)), ((), ()))


def dot(a, b, dims=NN, precision=None):
    return lax.dot_general(a, b, dims, precision=precision, preferred_element_type=F32)


def exact(a, b, dims=NN):
    return dot(a, b, dims, lax.Precision.HIGHEST)


def iota(shape, dim):
    return lax.broadcasted_iota(jnp.int32, shape, dim)


def block_base():
    return lax.axis_index(SEQ) * T


def doc_starts(len_ref):
    starts, at = [], jnp.int32(0)
    for d in range(DOCS):
        starts.append(at)
        at = at + len_ref[0, d]
    return starts


def segments(starts, base, offset):
    count = jnp.zeros(offset.shape, jnp.int32)
    for s in starts:
        local = jnp.where(s >= base, s - base, jnp.int32(1 << 20))
        count = count + (offset >= local).astype(jnp.int32)
    return count


def end_count(starts, base):
    count = jnp.int32(0)
    for s in starts:
        count = count + jnp.logical_and(s >= base, s < base + T).astype(jnp.int32)
    return count


def lower_triangle():
    return (iota((T, T), 1) <= iota((T, T), 0)).astype(F32)


def weights(ld, starts, base):
    log_cum = exact(lower_triangle(), ld, NT)
    seg = segments(starts, base, iota((T, HEADS), 0))
    last = end_count(starts, base)
    log_end = log_cum[T - 1 :, :]
    w_end = jnp.where(seg == last, jnp.exp(log_end - log_cum), 0.0)
    w_start = jnp.where(seg == 0, jnp.exp(log_cum), 0.0)
    gain = jnp.exp(log_end) * (last == 0).astype(F32)
    return w_end, w_start, gain


def spread(w, j, low):
    return jnp.where(low, w[:, 2 * j : 2 * j + 1], w[:, 2 * j + 1 : 2 * j + 2])


def cols(j):
    return slice(j * 128, (j + 1) * 128)


def heads_of(rows):
    lane = iota((PAIRS, 128), 1)
    row = iota((PAIRS, 128), 0)
    even = jnp.sum(jnp.where(lane < 64, rows, 0.0), axis=1, keepdims=True)
    odd = jnp.sum(jnp.where(lane < 64, 0.0, rows), axis=1, keepdims=True)
    placed = jnp.where(lane == 2 * row, even, jnp.where(lane == 2 * row + 1, odd, 0.0))
    return jnp.sum(placed, axis=0, keepdims=True)


def is_first():
    return lax.axis_index(CORE) == 0


def local_sums(roles_ref, slot, j, w, low, p_t):
    own = roles_ref[slot, :, cols(j)].astype(F32)
    return dot(p_t, (own * spread(w, j, low)).astype(BF16))


def prep_kernel(
    len_hbm, v_hbm, g_hbm, b_hbm, c_hbm, ld_hbm,
    roles_ref, rows_ref, w_ref, gain_ref, send_ref,
    len_ref, ld_ref, small_sems, v_sems, g_sems,
):
    first = is_first()
    v_slot = jnp.where(first, 1, 0)
    g_slot = 1 - v_slot
    small = [
        pltpu.make_async_copy(len_hbm, len_ref, small_sems.at[0]),
        pltpu.make_async_copy(ld_hbm.at[0], ld_ref, small_sems.at[1]),
        pltpu.make_async_copy(b_hbm.at[0], rows_ref.at[v_slot], small_sems.at[2]),
        pltpu.make_async_copy(c_hbm.at[0], rows_ref.at[g_slot], small_sems.at[3]),
    ]
    for copy in small:
        copy.start()
    wide = []
    for k in range(PARTS):
        part = slice(k * PART, (k + 1) * PART)
        vc = pltpu.make_async_copy(
            v_hbm.at[0, :, part], roles_ref.at[v_slot, :, part], v_sems.at[k]
        )
        gc = pltpu.make_async_copy(
            g_hbm.at[0, :, part], roles_ref.at[g_slot, :, part], g_sems.at[k]
        )
        vc.start()
        gc.start()
        wide.append((vc, gc))
    for copy in small:
        copy.wait()
    starts = doc_starts(len_ref)
    w_end, w_start, gain = weights(ld_ref[...], starts, block_base())
    w = jnp.where(first, w_start, w_end)
    w_ref[0] = w
    w_ref[1] = jnp.where(first, w_end, w_start)
    p_t = rows_ref[0].T
    low = iota((T, 128), 1) < 64
    skips = []
    for j in range(PAIRS):
        if j % (PAIRS // PARTS) == 0:
            for copy in wide[j // (PAIRS // PARTS)]:
                copy.wait()
        gain_ref[j : j + 1] = spread(gain, j, low[:1])
        both = roles_ref[0, :, cols(j)].astype(F32) * roles_ref[1, :, cols(j)].astype(F32)
        skips.append(jnp.sum(both, axis=0, keepdims=True))
        send_ref[j, :N] = local_sums(roles_ref, 0, j, w, low, p_t)
    skip = heads_of(jnp.concatenate(skips, axis=0))
    sub = iota((EXT, 128), 0)
    for j in range(PAIRS):
        send_ref[j, N:] = jnp.where(sub == 0, gain_ref[j : j + 1], jnp.where(sub == 1, skip, 0.0))


def own_kernel(
    _, len_ref, skip_gain_ref, roles_ref, rows_ref, w_ref, mine_ref, keep_ref, gains_ref
):
    low = iota((T, 128), 1) < 64
    p_t = rows_ref[1].T
    w = w_ref[1]
    for j in range(PAIRS):
        mine_ref[j] = local_sums(roles_ref, 1, j, w, low, p_t)
        gains_ref[j : j + 1] = jnp.where(
            low[:1], skip_gain_ref[2 * j], skip_gain_ref[2 * j + 1]
        )
    base = block_base()
    starts = doc_starts(len_ref)
    offset = iota((EXT, T), 1)
    keep = jnp.ones((EXT, T), F32)
    for s in starts:
        keep = jnp.where(offset + base == s, 0.0, keep)
    keep_ref[...] = keep


def combine_kernel(recv_ref, mine_ref, send_ref, out_ref):
    sub = iota((EXT, 128), 0)
    for j in range(PAIRS):
        theirs = recv_ref[j, N:]
        ours = send_ref[j, N:]
        out_ref[j, :N] = theirs[:1] * mine_ref[j] + recv_ref[j, :N]
        out_ref[j, N:] = jnp.where(sub == 0, theirs * ours, theirs + ours)


def scan_kernel(in_ref, skip_ref, out_ref, buffer, sems):
    first = is_first()
    running = jnp.zeros((N, 128), F32)
    skip = jnp.zeros((EXT, 128), F32)
    copies = []
    for i in range(PAIRS):
        at = jnp.where(first, i, PAIRS - 1 - i)
        buffer[i] = running
        copies.append(pltpu.make_async_copy(buffer.at[i], out_ref.at[at], sems.at[i]))
        copies[-1].start()
        if i < PAIRS - 1:
            running = in_ref[at, N : N + 1] * running + in_ref[at, :N]
        skip = skip + in_ref[i, N:]
    skip_ref[...] = jnp.broadcast_to(skip[1:2], (EXT, 128))
    for copy in copies:
        copy.wait()


def inside_kernel(_, len_ref, roles_ref, rows_ref, ld_ref, part_ref, raw_ref):
    first = is_first()
    v_slot = jnp.where(first, 1, 0)
    g_slot = 1 - v_slot
    base = block_base()
    starts = doc_starts(len_ref)
    ld = ld_ref[0]
    tri = lower_triangle()
    cum_t = exact(tri, ld, NT)
    cum_h = exact(ld, tri, NT)
    t_at = iota((T, T), 0)
    s_at = iota((T, T), 1)
    same = segments(starts, base, t_at) == segments(starts, base, s_at)
    bias = jnp.where(jnp.logical_and(s_at <= t_at, same), 0.0, FAR)
    b = rows_ref[v_slot]
    c = rows_ref[g_slot]
    scores = dot(c, b, NT)
    low = iota((T, 128), 1) < 64
    zero = jnp.zeros((T, 128), BF16)
    grad_scores = jnp.zeros((T, T), F32)
    for j in range(PAIRS):
        v = roles_ref[v_slot, :, cols(j)]
        g = roles_ref[g_slot, :, cols(j)]
        v_two = jnp.concatenate([jnp.where(low, v, zero), jnp.where(low, zero, v)], axis=0)
        g_two = jnp.concatenate([jnp.where(low, g, zero), jnp.where(low, zero, g)], axis=0)
        grad_mix = dot(g, v_two, NT)
        mixes = []
        for k in range(2):
            h = 2 * j + k
            decay = jnp.exp(cum_t[:, h : h + 1] - cum_h[h : h + 1, :] + bias)
            mixes.append((scores * decay).astype(BF16))
            grad_scores = grad_scores + grad_mix[:, k * T : (k + 1) * T] * decay
        part_ref[g_slot, :, cols(j)] = dot(jnp.concatenate(mixes, axis=1), v_two)
        part_ref[v_slot, :, cols(j)] = dot(jnp.concatenate(mixes, axis=0), g_two, TN)
    half = grad_scores.astype(BF16)
    raw_ref[g_slot] = dot(half, b)
    raw_ref[v_slot] = dot(half, c, TN)


def pass_on_kernel(_, x_ref, mine_ref, gain_ref, s0_ref, s1_ref, s2_ref, s3_ref, out_ref):
    for j in range(PAIRS):
        out_ref[j * N : (j + 1) * N] = gain_ref[j : j + 1] * x_ref[j] + mine_ref[j]
    sub = iota((EXT, 128), 0)
    plane = lax.axis_index("dp") + 4 * lax.axis_index(CORE)
    ext = jnp.zeros((EXT, 128), F32)
    for k, ref in enumerate((s0_ref, s1_ref, s2_ref, s3_ref)):
        ext = jnp.where(sub == ((plane + k) & 7), ref[...], ext)
    out_ref[PAIRS * N :] = ext


def finish_role(slot, j, low, x, roles_ref, rows, w, part_ref, skip_gains):
    half = x.astype(BF16)
    own = roles_ref[slot, :, cols(j)].astype(F32)
    skipped = roles_ref[1 - slot, :, cols(j)].astype(F32)
    wide = spread(w, j, low)
    tail = wide * dot(rows, half)
    out = part_ref[slot, :, cols(j)] + tail
    result = (out + skip_gains[j : j + 1] * skipped).astype(BF16)
    change = own * out
    hi = change.astype(BF16)
    lo = (change - hi.astype(F32)).astype(BF16)
    lane = iota((128, 128), 0)
    head = iota((128, 128), 1)
    pick = (head == 2 * j + jnp.where(lane < 64, 0, 1)).astype(BF16)
    end = jnp.sum(own * tail, axis=0, keepdims=True)
    return result, dot(hi, pick) + dot(lo, pick), end, dot((own * wide).astype(BF16), half, NT)


def near_kernel(
    _, x_ref, roles_ref, rows_ref, w_ref, part_ref, raw_ref, gains_ref,
    out_ref, total_ref, change_ref, end_ref,
):
    low = iota((T, 128), 1) < 64
    rows = rows_ref[0]
    w = w_ref[0]
    skip_gains = gains_ref[...]
    total = raw_ref[0]
    changes = jnp.zeros((T, 128), F32)
    for j in range(PAIRS):
        result, change, end, more = finish_role(
            0, j, low, x_ref[j], roles_ref, rows, w, part_ref, skip_gains
        )
        out_ref[:, cols(j)] = result
        changes = changes + change
        total = total + more
        end_ref[j : j + 1] = end
    total_ref[...] = total
    change_ref[...] = changes


def far_kernel(
    scales, y_ref, x_ref, passed_ref, roles_ref, rows_ref, w_ref, part_ref, raw_ref, gains_ref,
    gain_ref, keep_ref, near_ref, near_total_ref, near_change_ref, near_end_ref,
    igrad_ref, ograd_ref, dgrad_ref, skip_ref, mixed_hbm, vgrad_hbm,
    mixed_ref, vgrad_ref, sems,
):
    in_scale, out_scale, decay_scale, skip_scale = scales
    first = is_first()
    low = iota((T, 128), 1) < 64
    rows = rows_ref[1]
    w = w_ref[1]
    skip_gains = gains_ref[...]
    total = raw_ref[1]
    changes = near_change_ref[...]
    ends = []
    copies = []
    for j in range(PAIRS):
        y = y_ref[j * N : (j + 1) * N]
        result, change, end, more = finish_role(
            1, j, low, y, roles_ref, rows, w, part_ref, skip_gains
        )
        near = near_ref[:, cols(j)]
        mixed_ref[:, cols(j)] = jnp.where(first, near, result)
        vgrad_ref[:, cols(j)] = jnp.where(first, result, near)
        if (j + 1) % (PAIRS // PARTS) == 0:
            k = j // (PAIRS // PARTS)
            part = slice(k * PART, (k + 1) * PART)
            for n, (src, dst) in enumerate(((mixed_ref, mixed_hbm), (vgrad_ref, vgrad_hbm))):
                copies.append(
                    pltpu.make_async_copy(src.at[:, part], dst.at[0, :, part], sems.at[n, k])
                )
                copies[-1].start()
        changes = changes - change
        total = total + more
        meet = jnp.sum(x_ref[j] * y, axis=0, keepdims=True)
        end = jnp.where(first, end, near_end_ref[j : j + 1])
        ends.append(end + gain_ref[j : j + 1] * meet)
    near_total = near_total_ref[...]
    igrad_ref[0] = jnp.where(first, total, near_total) * in_scale
    ograd_ref[0] = jnp.where(first, near_total, total) * out_scale
    changes = jnp.where(first, changes, -changes)
    at_end = iota((T, 128), 0) == T - 1
    changes = changes + jnp.where(at_end, heads_of(jnp.concatenate(ends, axis=0)), 0.0)
    summed = exact(changes, lower_triangle(), TN)[:HEADS]
    dgrad_ref[0] = summed * keep_ref[:1] * decay_scale
    skips = passed_ref[PAIRS * N :] + y_ref[PAIRS * N :]
    skip_ref[...] = jnp.sum(skips, axis=0, keepdims=True)[:, :HEADS] * skip_scale
    for copy in copies:
        copy.wait()


def call(kernel, outs, *args, after=(), spaces=(), out_spaces=(), scratch=(), flops=0, moved=0):
    in_specs = [ANY] * len(after) + list(spaces)
    in_specs += [VMEM] * (len(args) + len(after) - len(in_specs))
    out_specs = [VMEM] * (len(outs) - len(out_spaces)) + list(out_spaces)
    return pl.pallas_call(
        kernel,
        out_shape=tuple(outs),
        in_specs=in_specs,
        out_specs=tuple(out_specs),
        scratch_shapes=list(scratch),
        compiler_params=pltpu.CompilerParams(vmem_limit_bytes=16 << 20),
        cost_estimate=pl.CostEstimate(flops=flops, bytes_accessed=moved, transcendentals=0),
    )(*after, *args)


def f32(*shape):
    return jax.ShapeDtypeStruct(shape, F32)


def bf16(*shape):
    return jax.ShapeDtypeStruct(shape, BF16)


def dma(*shape):
    return pltpu.SemaphoreType.DMA(shape)


def swap_cores(x):
    return lax.ppermute(x, CORE, [(0, 1), (1, 0)])


def exchange(x):
    return lax.all_to_all(x, CHIPS, split_axis=0, concat_axis=0, tiled=True)


def from_plane(x, offset):
    pairs = []
    for d in range(8):
        for c in range(2):
            pairs.append((((d + 4 * c + offset) % 8) * 2 + c, d * 2 + c))
    return lax.ppermute(x, ("dp", CORE), pairs)


def body(values_in, input_proj, output_proj, log_decay, doc_lengths, skip_gain, out_cotangent):
    inputs = (doc_lengths, values_in, out_cotangent, input_proj, output_proj, log_decay)
    token_count = lax.axis_size(SEQ) * T
    seq_count = lax.axis_size("dp")
    inner = values_in.shape[2]
    head_dim = inner // HEADS
    loaded = f32(PAIRS, N + EXT, 128)
    plain = f32(PAIRS, N, 128)
    roles, rows, w, gain, send = call(
        prep_kernel,
        (bf16(2, T, inner), bf16(2, T, N), f32(2, T, HEADS), f32(PAIRS, 128), loaded),
        *(pltpu.with_memory_space_constraint(a, pltpu.HBM) for a in inputs),
        spaces=[HBM] * 6,
        scratch=[
            pltpu.SMEM((1, DOCS), jnp.int32), pltpu.VMEM((HEADS, T), F32),
            dma(4), dma(PARTS), dma(PARTS),
        ],
        moved=4 << 20,
    )
    recv = swap_cores(send)
    mine, keep, gains = call(
        own_kernel,
        (plain, f32(EXT, T), f32(PAIRS, 128)),
        doc_lengths, skip_gain, roles, rows, w,
        after=(send,),
        spaces=[SMEM] * 2,
        moved=4 << 20,
    )
    (chip,) = call(combine_kernel, (loaded,), recv, mine, send, moved=3 << 20)
    gathered = exchange(chip)
    skip, prefix = call(
        scan_kernel,
        (f32(EXT, 128), plain),
        gathered,
        out_spaces=[HBM],
        scratch=[pltpu.VMEM((PAIRS, N, 128), F32), dma(PAIRS)],
        moved=2 << 20,
    )
    x = exchange(prefix)
    skips = [from_plane(skip, k) for k in range(4)]
    part, raw = call(
        inside_kernel,
        (f32(2, T, inner), f32(2, T, N)),
        doc_lengths, roles, rows, log_decay,
        after=(prefix,),
        spaces=[SMEM],
        moved=12 << 20,
    )
    (passed,) = call(
        pass_on_kernel,
        (f32(PAIRS * N + EXT, 128),),
        x, mine, gain, *skips,
        after=(raw,),
        moved=3 << 20,
    )
    y = swap_cores(passed)
    near = call(
        near_kernel,
        (bf16(T, inner), f32(T, N), f32(T, 128), f32(PAIRS, 128)),
        x, roles, rows, w, part, raw, gains,
        after=(passed,),
        moved=8 << 20,
    )
    scales = (
        1.0 / inner**0.5,
        (N / (inner * token_count)) ** 0.5,
        1.0 / (head_dim * token_count) ** 0.5,
        1.0 / (seq_count * token_count * head_dim) ** 0.5,
    )
    input_grad, output_grad, decay_grad, skip_grad, mixed, values_grad = call(
        functools.partial(far_kernel, scales),
        (
            f32(1, T, N), f32(1, T, N), f32(1, HEADS, T), f32(1, HEADS),
            bf16(1, T, inner), bf16(1, T, inner),
        ),
        y, x, passed, roles, rows, w, part, raw, gains, gain, keep, *near,
        out_spaces=[HBM] * 2,
        scratch=[pltpu.VMEM((T, inner), BF16), pltpu.VMEM((T, inner), BF16), dma(2, PARTS)],
        moved=8 << 20,
    )
    return mixed, values_grad, input_grad, output_grad, decay_grad, skip_grad[0]


def solution(mesh):
    finer = Mesh(mesh.devices.reshape(mesh.shape["dp"], 4, 4, 2), ("dp",) + SEQ)
    placed = (
        P("dp", SEQ, None),
        P("dp", SEQ, None),
        P("dp", SEQ, None),
        P("dp", None, SEQ),
        P("dp", None),
        P(),
        P("dp", SEQ, None),
    )
    return jax.shard_map(
        body,
        mesh=finer,
        in_specs=placed,
        out_specs=(
            P("dp", SEQ, None),
            P("dp", SEQ, None),
            P("dp", SEQ, None),
            P("dp", SEQ, None),
            P("dp", None, SEQ),
            P(),
        ),
        check_vma=False,
    )
```

```python
import functools

import jax
import jax.numpy as jnp
from jax import lax
from jax.experimental import pallas as pl
from jax.experimental.pallas import tpu as pltpu
from jax.sharding import Mesh
from jax.sharding import PartitionSpec as P


SEQ = ("seq_0", "seq_1", "seq_2")
CHIPS = ("seq_0", "seq_1")
CORE = "seq_2"
F32 = jnp.float32
BF16 = jnp.bfloat16
T = 128
N = 128
PAIRS = 16
HEADS = 32
DOCS = 8
EXT = 8
PARTS = 4
PART = 512
FAR = -1e30
VMEM = pl.BlockSpec(memory_space=pltpu.VMEM)
SMEM = pl.BlockSpec(memory_space=pltpu.SMEM)
ANY = pl.BlockSpec(memory_space=pl.ANY)
HBM = pl.BlockSpec(memory_space=pltpu.HBM)

NN = (((1,), (0,)), ((), ()))
NT = (((1,), (1,)), ((), ()))
TN = (((0,), (0,)), ((), ()))


def dot(a, b, dims=NN, precision=None):
    return lax.dot_general(a, b, dims, precision=precision, preferred_element_type=F32)


def thirds(a):
    high = a.astype(BF16)
    rest = a - high.astype(F32)
    middle = rest.astype(BF16)
    return high, middle, (rest - middle.astype(F32)).astype(BF16)


def add_up(pieces):
    return functools.reduce(lambda a, b: a + b, pieces)


def iota(shape, dim):
    return lax.broadcasted_iota(jnp.int32, shape, dim)


def block_base():
    return lax.axis_index(SEQ) * T


def doc_starts(len_ref):
    starts, at = [], jnp.int32(0)
    for d in range(DOCS):
        starts.append(at)
        at = at + len_ref[0, d]
    return starts


def segments(starts, base, offset):
    count = jnp.zeros(offset.shape, jnp.int32)
    for s in starts:
        local = jnp.where(s >= base, s - base, jnp.int32(1 << 20))
        count = count + (offset >= local).astype(jnp.int32)
    return count


def end_count(starts, base):
    count = jnp.int32(0)
    for s in starts:
        count = count + jnp.logical_and(s >= base, s < base + T).astype(jnp.int32)
    return count


def lower_triangle():
    return (iota((T, T), 1) <= iota((T, T), 0)).astype(BF16)


def weights(ld, starts, base):
    tri = lower_triangle()
    log_cum = add_up(dot(tri, third, NT) for third in thirds(ld))
    seg = segments(starts, base, iota((T, HEADS), 0))
    last = end_count(starts, base)
    log_end = log_cum[T - 1 :, :]
    w_end = jnp.where(seg == last, jnp.exp(log_end - log_cum), 0.0)
    w_start = jnp.where(seg == 0, jnp.exp(log_cum), 0.0)
    gain = jnp.exp(log_end) * (last == 0).astype(F32)
    return w_end, w_start, gain


def spread(w, j, low):
    return jnp.where(low, w[:, 2 * j : 2 * j + 1], w[:, 2 * j + 1 : 2 * j + 2])


def cols(j):
    return slice(j * 128, (j + 1) * 128)


def heads_of(rows):
    lane = iota((PAIRS, 128), 1)
    row = iota((PAIRS, 128), 0)
    even = jnp.sum(jnp.where(lane < 64, rows, 0.0), axis=1, keepdims=True)
    odd = jnp.sum(jnp.where(lane < 64, 0.0, rows), axis=1, keepdims=True)
    placed = jnp.where(lane == 2 * row, even, jnp.where(lane == 2 * row + 1, odd, 0.0))
    return jnp.sum(placed, axis=0, keepdims=True)


def is_first():
    return lax.axis_index(CORE) == 0


def local_sums(roles_ref, slot, j, w, low, p_t):
    own = roles_ref[slot, :, cols(j)].astype(F32)
    return dot(p_t, (own * spread(w, j, low)).astype(BF16))


def prep_kernel(
    len_hbm, v_hbm, g_hbm, b_hbm, c_hbm, ld_hbm,
    roles_ref, rows_ref, w_ref, gain_ref, send_ref,
    len_ref, ld_ref, small_sems, v_sems, g_sems,
):
    first = is_first()
    v_slot = jnp.where(first, 1, 0)
    g_slot = 1 - v_slot
    small = [
        pltpu.make_async_copy(len_hbm, len_ref, small_sems.at[0]),
        pltpu.make_async_copy(ld_hbm.at[0], ld_ref, small_sems.at[1]),
        pltpu.make_async_copy(b_hbm.at[0], rows_ref.at[v_slot], small_sems.at[2]),
        pltpu.make_async_copy(c_hbm.at[0], rows_ref.at[g_slot], small_sems.at[3]),
    ]
    for copy in small:
        copy.start()
    wide = []
    for k in range(PARTS):
        part = slice(k * PART, (k + 1) * PART)
        vc = pltpu.make_async_copy(
            v_hbm.at[0, :, part], roles_ref.at[v_slot, :, part], v_sems.at[k]
        )
        gc = pltpu.make_async_copy(
            g_hbm.at[0, :, part], roles_ref.at[g_slot, :, part], g_sems.at[k]
        )
        vc.start()
        gc.start()
        wide.append((vc, gc))
    for copy in small:
        copy.wait()
    starts = doc_starts(len_ref)
    w_end, w_start, gain = weights(ld_ref[...], starts, block_base())
    w = jnp.where(first, w_start, w_end)
    w_ref[0] = w
    w_ref[1] = jnp.where(first, w_end, w_start)
    p_t = rows_ref[0].T
    low = iota((T, 128), 1) < 64
    skips = []
    for j in range(PAIRS):
        if j % (PAIRS // PARTS) == 0:
            for copy in wide[j // (PAIRS // PARTS)]:
                copy.wait()
        gain_ref[j : j + 1] = spread(gain, j, low[:1])
        both = roles_ref[0, :, cols(j)].astype(F32) * roles_ref[1, :, cols(j)].astype(F32)
        skips.append(jnp.sum(both, axis=0, keepdims=True))
        send_ref[j, :N] = local_sums(roles_ref, 0, j, w, low, p_t)
    skip = heads_of(jnp.concatenate(skips, axis=0))
    sub = iota((EXT, 128), 0)
    for j in range(PAIRS):
        send_ref[j, N:] = jnp.where(sub == 0, gain_ref[j : j + 1], jnp.where(sub == 1, skip, 0.0))


def own_kernel(
    _, len_ref, skip_gain_ref, roles_ref, rows_ref, w_ref, gain_ref, mine_ref, keep_ref, gains_ref
):
    low = iota((T, 128), 1) < 64
    p_t = rows_ref[1].T
    w = w_ref[1]
    for j in range(PAIRS):
        mine_ref[j, N:] = jnp.broadcast_to(gain_ref[j : j + 1], (EXT, 128))
        mine_ref[j, :N] = local_sums(roles_ref, 1, j, w, low, p_t)
        gains_ref[j : j + 1] = jnp.where(
            low[:1], skip_gain_ref[2 * j], skip_gain_ref[2 * j + 1]
        )
    base = block_base()
    starts = doc_starts(len_ref)
    offset = iota((EXT, T), 1)
    keep = jnp.ones((EXT, T), F32)
    for s in starts:
        keep = jnp.where(offset + base == s, 0.0, keep)
    keep_ref[...] = keep


def combine_kernel(recv_ref, mine_ref, send_ref, out_ref):
    sub = iota((EXT, 128), 0)
    for j in range(PAIRS):
        theirs = recv_ref[j, N:]
        ours = send_ref[j, N:]
        out_ref[j, :N] = theirs[:1] * mine_ref[j, :N] + recv_ref[j, :N]
        out_ref[j, N:] = jnp.where(sub == 0, theirs * ours, theirs + ours)


def scan_kernel(in_ref, skip_ref, out_ref, buffer, sems):
    first = is_first()
    running = jnp.zeros((N, 128), F32)
    skip = jnp.zeros((EXT, 128), F32)
    copies = []
    for i in range(PAIRS):
        at = jnp.where(first, i, PAIRS - 1 - i)
        buffer[i] = running
        copies.append(pltpu.make_async_copy(buffer.at[i], out_ref.at[at], sems.at[i]))
        copies[-1].start()
        if i < PAIRS - 1:
            running = in_ref[at, N : N + 1] * running + in_ref[at, :N]
        skip = skip + in_ref[i, N:]
    skip_ref[...] = jnp.broadcast_to(skip[1:2], (EXT, 128))
    for copy in copies:
        copy.wait()


def halves(x):
    high = x.astype(BF16)
    return high, (x - high.astype(F32)).astype(BF16)


def picked_sums(x, pick):
    high, low = halves(x)
    return dot(high, pick) + dot(low, pick)


def inside_kernel(
    len_ref, v_hbm, g_hbm, rows_ref, ld_ref, w_ref, gains_ref, skip_in_ref,
    raw_ref, change_ref, skip_ref, base_hbm, wide_hbm, wt_hbm, pick_hbm,
    roles_ref, base_ref, wide_ref, wt_ref, pick_ref, sems, in_sems,
):
    first = is_first()
    v_slot = jnp.where(first, 1, 0)
    g_slot = 1 - v_slot
    fetch = [
        pltpu.make_async_copy(v_hbm.at[0], roles_ref.at[v_slot], in_sems.at[0]),
        pltpu.make_async_copy(g_hbm.at[0], roles_ref.at[g_slot], in_sems.at[1]),
    ]
    for copy in fetch:
        copy.start()
    base = block_base()
    starts = doc_starts(len_ref)
    ld = ld_ref[0]
    tri = lower_triangle()
    cum_t = add_up(dot(tri, third, NT) for third in thirds(ld))
    cum_h = add_up(dot(third, tri, NT) for third in thirds(ld))
    t_at = iota((T, T), 0)
    s_at = iota((T, T), 1)
    same = segments(starts, base, t_at) == segments(starts, base, s_at)
    bias = jnp.where(jnp.logical_and(s_at <= t_at, same), 0.0, FAR)
    b = rows_ref[v_slot]
    c = rows_ref[g_slot]
    scores = dot(c, b, NT)
    low = iota((T, 128), 1) < 64
    zero = jnp.zeros((T, 128), BF16)
    grad_scores = jnp.zeros((T, T), F32)
    changes = jnp.zeros((T, 128), F32)
    head = iota((128, 128), 1) - (iota((128, 128), 0) >= 64).astype(jnp.int32)
    skip_ref[...] = skip_in_ref[...]
    copies = []
    for copy in fetch:
        copy.wait()
    for j in range(PAIRS):
        v = roles_ref[v_slot, :, cols(j)]
        g = roles_ref[g_slot, :, cols(j)]
        v_two = jnp.concatenate([jnp.where(low, v, zero), jnp.where(low, zero, v)], axis=0)
        g_two = jnp.concatenate([jnp.where(low, g, zero), jnp.where(low, zero, g)], axis=0)
        grad_mix = dot(g, v_two, NT)
        mixes = []
        for k in range(2):
            h = 2 * j + k
            decay = jnp.exp(cum_t[:, h : h + 1] - cum_h[h : h + 1, :] + bias)
            mixes.append((scores * decay).astype(BF16))
            grad_scores = grad_scores + grad_mix[:, k * T : (k + 1) * T] * decay
        within = dot(jnp.concatenate(mixes, axis=1), v_two)
        back = dot(jnp.concatenate(mixes, axis=0), g_two, TN)
        v = v.astype(F32)
        g = g.astype(F32)
        skip_row = gains_ref[j : j + 1]
        base_ref[g_slot, :, cols(j)] = within + skip_row * v
        base_ref[v_slot, :, cols(j)] = back + skip_row * g
        pick = (head == 2 * j).astype(BF16)
        pick_ref[cols(j)] = pick
        changes = changes + picked_sums(g * within - v * back, pick)
        for slot in range(2):
            wide = spread(w_ref[slot], j, low)
            wide_ref[slot, :, cols(j)] = wide
            own = roles_ref[slot, :, cols(j)].astype(F32)
            wt_ref[slot, :, cols(j)] = (own * wide).astype(BF16)
        if (j + 1) % (PAIRS // PARTS) == 0:
            k = j // (PAIRS // PARTS)
            part = slice(k * PART, (k + 1) * PART)
            pairs = ((base_ref, base_hbm), (wide_ref, wide_hbm), (wt_ref, wt_hbm))
            for n, (src, dst) in enumerate(pairs):
                copies.append(
                    pltpu.make_async_copy(
                        src.at[:, :, part], dst.at[:, :, part], sems.at[n, k]
                    )
                )
            copies.append(pltpu.make_async_copy(pick_ref.at[part], pick_hbm.at[part], sems.at[3, k]))
            for copy in copies[-4:]:
                copy.start()
    change_ref[...] = changes
    half = grad_scores.astype(BF16)
    raw_ref[g_slot] = dot(half, b)
    raw_ref[v_slot] = dot(half, c, TN)
    for copy in copies:
        copy.wait()


def pass_on_kernel(_, x_ref, mine_ref, s0_ref, s1_ref, s2_ref, s3_ref, out_ref, gain_ref):
    for j in range(PAIRS):
        gain = mine_ref[j, N : N + 1]
        gain_ref[j : j + 1] = gain
        out_ref[j * N : (j + 1) * N] = gain * x_ref[j] + mine_ref[j, :N]
    sub = iota((EXT, 128), 0)
    plane = lax.axis_index("dp") + 4 * lax.axis_index(CORE)
    ext = jnp.zeros((EXT, 128), F32)
    for k, ref in enumerate((s0_ref, s1_ref, s2_ref, s3_ref)):
        ext = jnp.where(sub == ((plane + k) & 7), ref[...], ext)
    out_ref[PAIRS * N :] = ext


def finish_role(x_of, rows, base_ref, wide_ref, wt_ref, work, before, emit):
    half_ref, hi_ref, lo_ref = work
    for j in range(PAIRS):
        before(j)
        half = x_of(j).astype(BF16)
        half_ref[:, cols(j)] = half
        read = dot(rows, half)
        tail = wide_ref[:, cols(j)] * read
        change = wt_ref[:, cols(j)].astype(F32) * read
        hi_ref[:, cols(j)], lo_ref[:, cols(j)] = halves(change)
        emit(
            j,
            (base_ref[:, cols(j)] + tail).astype(BF16),
            jnp.sum(change, axis=0, keepdims=True),
        )


def near_kernel(
    _, x_ref, rows_ref, raw_ref, base_hbm, wide_hbm, wt_hbm, pick_hbm,
    out_ref, total_ref, change_ref, end_ref, pick_ref, base_far, wide_far, wt_far,
    base_ref, wide_ref, wt_ref, half_ref, hi_ref, lo_ref, sems, far_sems,
):
    parts = []
    for k in range(PARTS):
        part = slice(k * PART, (k + 1) * PART)
        parts.append(
            (
                pltpu.make_async_copy(
                    base_hbm.at[0, :, part], base_ref.at[:, part], sems.at[0, k]
                ),
                pltpu.make_async_copy(
                    wide_hbm.at[0, :, part], wide_ref.at[:, part], sems.at[1, k]
                ),
                pltpu.make_async_copy(
                    wt_hbm.at[0, :, part], wt_ref.at[:, part], sems.at[2, k]
                ),
            )
        )
        for copy in parts[-1]:
            copy.start()
    later = [
        pltpu.make_async_copy(pick_hbm, pick_ref, far_sems.at[0]),
        pltpu.make_async_copy(base_hbm.at[1], base_far, far_sems.at[1]),
        pltpu.make_async_copy(wide_hbm.at[1], wide_far, far_sems.at[2]),
        pltpu.make_async_copy(wt_hbm.at[1], wt_far, far_sems.at[3]),
    ]
    for copy in later:
        copy.start()

    def before(j):
        if j % (PAIRS // PARTS) == 0:
            for copy in parts[j // (PAIRS // PARTS)]:
                copy.wait()

    def emit(j, result, end):
        out_ref[:, cols(j)] = result
        end_ref[j : j + 1] = end

    work = (half_ref, hi_ref, lo_ref)
    finish_role(
        lambda j: x_ref[j], rows_ref[0], base_ref, wide_ref, wt_ref, work, before, emit
    )
    later[0].wait()
    total_ref[...] = raw_ref[0] + dot(wt_ref[...], half_ref[...], NT)
    pick = pick_ref[...]
    change_ref[...] = dot(hi_ref[...], pick) + dot(lo_ref[...], pick)
    for copy in later[1:]:
        copy.wait()


def far_kernel(
    scales, y_ref, x_ref, passed_ref, rows_ref, raw_ref, base_change_ref, gain_ref,
    keep_ref, near_ref, near_total_ref, near_change_ref, near_end_ref, pick_ref, base_ref,
    wide_ref, wt_ref,
    skip_ref, igrad_hbm, ograd_hbm, dgrad_hbm, mixed_hbm, vgrad_hbm,
    mixed_ref, vgrad_ref, igrad_ref, ograd_ref, dgrad_ref, sems, small_sems,
    half_ref, hi_ref, lo_ref,
):
    in_scale, out_scale, decay_scale, skip_scale = scales
    first = is_first()
    copies = []
    ends = []

    def emit(j, result, end):
        near = near_ref[:, cols(j)]
        mixed_ref[:, cols(j)] = jnp.where(first, near, result)
        vgrad_ref[:, cols(j)] = jnp.where(first, result, near)
        meet = jnp.sum(x_ref[j] * y_ref[j * N : (j + 1) * N], axis=0, keepdims=True)
        end = jnp.where(first, end, near_end_ref[j : j + 1])
        ends.append(end + gain_ref[j : j + 1] * meet)
        if (j + 1) % (PAIRS // PARTS) == 0:
            k = j // (PAIRS // PARTS)
            part = slice(k * PART, (k + 1) * PART)
            for n, (src, dst) in enumerate(((mixed_ref, mixed_hbm), (vgrad_ref, vgrad_hbm))):
                copies.append(
                    pltpu.make_async_copy(src.at[:, part], dst.at[0, :, part], sems.at[n, k])
                )
                copies[-1].start()

    work = (half_ref, hi_ref, lo_ref)
    finish_role(
        lambda j: y_ref[j * N : (j + 1) * N], rows_ref[1], base_ref, wide_ref, wt_ref, work,
        lambda j: None, emit,
    )
    total = raw_ref[1] + dot(wt_ref[...], half_ref[...], NT)
    near_total = near_total_ref[...]
    igrad_ref[...] = jnp.where(first, total, near_total) * in_scale
    ograd_ref[...] = jnp.where(first, near_total, total) * out_scale
    small = [
        pltpu.make_async_copy(igrad_ref, igrad_hbm.at[0], small_sems.at[0]),
        pltpu.make_async_copy(ograd_ref, ograd_hbm.at[0], small_sems.at[1]),
        pltpu.make_async_copy(dgrad_ref, dgrad_hbm.at[0], small_sems.at[2]),
    ]
    small[0].start()
    small[1].start()
    pick = pick_ref[...]
    changes = near_change_ref[...] - (dot(hi_ref[...], pick) + dot(lo_ref[...], pick))
    changes = base_change_ref[...] + jnp.where(first, changes, -changes)
    at_end = iota((T, 128), 0) == T - 1
    changes = changes + jnp.where(at_end, heads_of(jnp.concatenate(ends, axis=0)), 0.0)
    tri = lower_triangle()
    summed = add_up(dot(third, tri, TN) for third in thirds(changes))[:HEADS]
    dgrad_ref[...] = summed * keep_ref[:1] * decay_scale
    small[2].start()
    skips = passed_ref[PAIRS * N :] + y_ref[PAIRS * N :]
    skip_ref[...] = jnp.sum(skips, axis=0, keepdims=True)[:, :HEADS] * skip_scale
    for copy in copies + small:
        copy.wait()


def call(kernel, outs, *args, after=(), spaces=(), out_spaces=(), scratch=(), flops=0, moved=0):
    in_specs = [ANY] * len(after) + list(spaces)
    in_specs += [VMEM] * (len(args) + len(after) - len(in_specs))
    out_specs = [VMEM] * (len(outs) - len(out_spaces)) + list(out_spaces)
    return pl.pallas_call(
        kernel,
        out_shape=tuple(outs),
        in_specs=in_specs,
        out_specs=tuple(out_specs),
        scratch_shapes=list(scratch),
        compiler_params=pltpu.CompilerParams(vmem_limit_bytes=20 << 20),
        cost_estimate=pl.CostEstimate(flops=flops, bytes_accessed=moved, transcendentals=0),
    )(*after, *args)


def f32(*shape):
    return jax.ShapeDtypeStruct(shape, F32)


def bf16(*shape):
    return jax.ShapeDtypeStruct(shape, BF16)


def dma(*shape):
    return pltpu.SemaphoreType.DMA(shape)


def swap_cores(x):
    return lax.ppermute(x, CORE, [(0, 1), (1, 0)])


def exchange(x):
    return lax.all_to_all(x, CHIPS, split_axis=0, concat_axis=0, tiled=True)


def from_plane(x, offset):
    pairs = []
    for d in range(8):
        for c in range(2):
            pairs.append((((d + 4 * c + offset) % 8) * 2 + c, d * 2 + c))
    return lax.ppermute(x, ("dp", CORE), pairs)


def body(values_in, input_proj, output_proj, log_decay, doc_lengths, skip_gain, out_cotangent):
    inputs = (doc_lengths, values_in, out_cotangent, input_proj, output_proj, log_decay)
    token_count = lax.axis_size(SEQ) * T
    seq_count = lax.axis_size("dp")
    inner = values_in.shape[2]
    head_dim = inner // HEADS
    loaded = f32(PAIRS, N + EXT, 128)
    plain = f32(PAIRS, N, 128)
    roles, rows, w, gain, send = call(
        prep_kernel,
        (bf16(2, T, inner), bf16(2, T, N), f32(2, T, HEADS), f32(PAIRS, 128), loaded),
        *(pltpu.with_memory_space_constraint(a, pltpu.HBM) for a in inputs),
        spaces=[HBM] * 6,
        scratch=[
            pltpu.SMEM((1, DOCS), jnp.int32), pltpu.VMEM((HEADS, T), F32),
            dma(4), dma(PARTS), dma(PARTS),
        ],
        moved=4 << 20,
    )
    recv = swap_cores(send)
    mine, keep, gains = call(
        own_kernel,
        (loaded, f32(EXT, T), f32(PAIRS, 128)),
        doc_lengths, skip_gain, roles, rows, w, gain,
        after=(send,),
        spaces=[SMEM] * 2,
        moved=4 << 20,
    )
    (chip,) = call(combine_kernel, (loaded,), recv, mine, send, moved=3 << 20)
    gathered = exchange(chip)
    skip, prefix = call(
        scan_kernel,
        (f32(EXT, 128), pltpu.HBM((PAIRS, N, 128), F32)),
        gathered,
        out_spaces=[HBM],
        scratch=[pltpu.VMEM((PAIRS, N, 128), F32), dma(PAIRS)],
        moved=2 << 20,
    )
    x = exchange(prefix)
    wide16 = pltpu.VMEM((T, inner), BF16)
    wide32 = pltpu.VMEM((T, inner), F32)
    raw, change, skip, *factors = call(
        inside_kernel,
        (
            f32(2, T, N), f32(T, 128), f32(EXT, 128), pltpu.HBM((2, T, inner), F32),
            pltpu.HBM((2, T, inner), F32), pltpu.HBM((2, T, inner), BF16),
            pltpu.HBM((inner, 128), BF16),
        ),
        doc_lengths,
        *(pltpu.with_memory_space_constraint(a, pltpu.HBM) for a in (values_in, out_cotangent)),
        rows, log_decay, w, gains, skip,
        spaces=[SMEM, HBM, HBM],
        out_spaces=[HBM] * 4,
        scratch=[
            pltpu.VMEM((2, T, inner), BF16), pltpu.VMEM((2, T, inner), F32),
            pltpu.VMEM((2, T, inner), F32), pltpu.VMEM((2, T, inner), BF16),
            pltpu.VMEM((inner, 128), BF16), dma(4, PARTS), dma(2),
        ],
        moved=12 << 20,
    )
    skips = [from_plane(skip, k) for k in range(4)]
    passed, gain = call(
        pass_on_kernel,
        (f32(PAIRS * N + EXT, 128), f32(PAIRS, 128)),
        x, mine, *skips,
        after=(raw,),
        moved=3 << 20,
    )
    y = swap_cores(passed)
    near = call(
        near_kernel,
        (
            bf16(T, inner), f32(T, N), f32(T, 128), f32(PAIRS, 128), bf16(inner, 128),
            f32(T, inner), f32(T, inner), bf16(T, inner),
        ),
        x, rows, raw,
        *(pltpu.with_memory_space_constraint(a, pltpu.HBM) for a in factors),
        after=(passed,),
        spaces=[VMEM] * 3 + [HBM] * 4,
        scratch=[wide32, wide32, wide16, wide16, wide16, wide16, dma(3, PARTS), dma(4)],
        moved=8 << 20,
    )
    scales = (
        1.0 / inner**0.5,
        (N / (inner * token_count)) ** 0.5,
        1.0 / (head_dim * token_count) ** 0.5,
        1.0 / (seq_count * token_count * head_dim) ** 0.5,
    )
    skip_grad, input_grad, output_grad, decay_grad, mixed, values_grad = call(
        functools.partial(far_kernel, scales),
        (
            f32(1, HEADS), f32(1, T, N), f32(1, T, N), f32(1, HEADS, T),
            bf16(1, T, inner), bf16(1, T, inner),
        ),
        y, x, passed, rows, raw, change, gain, keep, *near,
        out_spaces=[HBM] * 5,
        scratch=[
            wide16, wide16, pltpu.VMEM((T, N), F32), pltpu.VMEM((T, N), F32),
            pltpu.VMEM((HEADS, T), F32), dma(2, PARTS), dma(3), wide16, wide16, wide16,
        ],
        moved=8 << 20,
    )
    return mixed, values_grad, input_grad, output_grad, decay_grad, skip_grad[0]


def solution(mesh):
    finer = Mesh(mesh.devices.reshape(mesh.shape["dp"], 4, 4, 2), ("dp",) + SEQ)
    placed = (
        P("dp", SEQ, None),
        P("dp", SEQ, None),
        P("dp", SEQ, None),
        P("dp", None, SEQ),
        P("dp", None),
        P(),
        P("dp", SEQ, None),
    )
    return jax.shard_map(
        body,
        mesh=finer,
        in_specs=placed,
        out_specs=(
            P("dp", SEQ, None),
            P("dp", SEQ, None),
            P("dp", SEQ, None),
            P("dp", SEQ, None),
            P("dp", None, SEQ),
            P(),
        ),
        check_vma=False,
    )
```

```python
import functools

import jax
import jax.numpy as jnp
from jax import lax
from jax.experimental import pallas as pl
from jax.experimental.pallas import tpu as pltpu
from jax.sharding import Mesh
from jax.sharding import PartitionSpec as P


SEQ = ("seq_0", "seq_1", "seq_2")
CHIPS = ("seq_0", "seq_1")
CORE = "seq_2"
F32 = jnp.float32
BF16 = jnp.bfloat16
T = 128
N = 128
PAIRS = 16
HEADS = 32
DOCS = 8
EXT = 8
PARTS = 4
PART = 512
FAR = -1e30
VMEM = pl.BlockSpec(memory_space=pltpu.VMEM)
SMEM = pl.BlockSpec(memory_space=pltpu.SMEM)
ANY = pl.BlockSpec(memory_space=pl.ANY)
HBM = pl.BlockSpec(memory_space=pltpu.HBM)

NN = (((1,), (0,)), ((), ()))
NT = (((1,), (1,)), ((), ()))
TN = (((0,), (0,)), ((), ()))


def dot(a, b, dims=NN, precision=None):
    return lax.dot_general(a, b, dims, precision=precision, preferred_element_type=F32)


def thirds(a):
    high = a.astype(BF16)
    rest = a - high.astype(F32)
    middle = rest.astype(BF16)
    return high, middle, (rest - middle.astype(F32)).astype(BF16)


def add_up(pieces):
    return functools.reduce(lambda a, b: a + b, pieces)


def iota(shape, dim):
    return lax.broadcasted_iota(jnp.int32, shape, dim)


def block_base():
    return lax.axis_index(SEQ) * T


def doc_starts(len_ref):
    starts, at = [], jnp.int32(0)
    for d in range(DOCS):
        starts.append(at)
        at = at + len_ref[0, d]
    return starts


def segments(starts, base, offset):
    count = jnp.zeros(offset.shape, jnp.int32)
    for s in starts:
        local = jnp.where(s >= base, s - base, jnp.int32(1 << 20))
        count = count + (offset >= local).astype(jnp.int32)
    return count


def end_count(starts, base):
    count = jnp.int32(0)
    for s in starts:
        count = count + jnp.logical_and(s >= base, s < base + T).astype(jnp.int32)
    return count


def lower_triangle():
    return (iota((T, T), 1) <= iota((T, T), 0)).astype(BF16)


def weights(ld, starts, base):
    tri = lower_triangle()
    log_cum = add_up(dot(tri, third, NT) for third in thirds(ld))
    seg = segments(starts, base, iota((T, HEADS), 0))
    last = end_count(starts, base)
    log_end = log_cum[T - 1 :, :]
    w_end = jnp.where(seg == last, jnp.exp(log_end - log_cum), 0.0)
    w_start = jnp.where(seg == 0, jnp.exp(log_cum), 0.0)
    gain = jnp.exp(log_end) * (last == 0).astype(F32)
    return w_end, w_start, gain


def spread(w, j, low):
    return jnp.where(low, w[:, 2 * j : 2 * j + 1], w[:, 2 * j + 1 : 2 * j + 2])


def cols(j):
    return slice(j * 128, (j + 1) * 128)


def heads_of(rows):
    lane = iota((PAIRS, 128), 1)
    row = iota((PAIRS, 128), 0)
    even = jnp.sum(jnp.where(lane < 64, rows, 0.0), axis=1, keepdims=True)
    odd = jnp.sum(jnp.where(lane < 64, 0.0, rows), axis=1, keepdims=True)
    placed = jnp.where(lane == 2 * row, even, jnp.where(lane == 2 * row + 1, odd, 0.0))
    return jnp.sum(placed, axis=0, keepdims=True)


def is_first():
    return lax.axis_index(CORE) == 0


def local_sums(roles_ref, slot, j, w, low, p_t):
    own = roles_ref[slot, :, cols(j)].astype(F32)
    return dot(p_t, (own * spread(w, j, low)).astype(BF16))


def prep_kernel(
    len_hbm, v_hbm, g_hbm, b_hbm, c_hbm, ld_hbm,
    roles_ref, rows_ref, w_ref, gain_ref, send_ref,
    len_ref, ld_ref, small_sems, v_sems, g_sems,
):
    first = is_first()
    v_slot = jnp.where(first, 1, 0)
    g_slot = 1 - v_slot
    small = [
        pltpu.make_async_copy(len_hbm, len_ref, small_sems.at[0]),
        pltpu.make_async_copy(ld_hbm.at[0], ld_ref, small_sems.at[1]),
        pltpu.make_async_copy(b_hbm.at[0], rows_ref.at[v_slot], small_sems.at[2]),
        pltpu.make_async_copy(c_hbm.at[0], rows_ref.at[g_slot], small_sems.at[3]),
    ]
    for copy in small:
        copy.start()
    wide = []
    for k in range(PARTS):
        part = slice(k * PART, (k + 1) * PART)
        vc = pltpu.make_async_copy(
            v_hbm.at[0, :, part], roles_ref.at[v_slot, :, part], v_sems.at[k]
        )
        gc = pltpu.make_async_copy(
            g_hbm.at[0, :, part], roles_ref.at[g_slot, :, part], g_sems.at[k]
        )
        vc.start()
        gc.start()
        wide.append((vc, gc))
    for copy in small:
        copy.wait()
    starts = doc_starts(len_ref)
    w_end, w_start, gain = weights(ld_ref[...], starts, block_base())
    w = jnp.where(first, w_start, w_end)
    w_ref[0] = w
    w_ref[1] = jnp.where(first, w_end, w_start)
    p_t = rows_ref[0].T
    low = iota((T, 128), 1) < 64
    skips = []
    for j in range(PAIRS):
        if j % (PAIRS // PARTS) == 0:
            for copy in wide[j // (PAIRS // PARTS)]:
                copy.wait()
        gain_ref[j : j + 1] = spread(gain, j, low[:1])
        both = roles_ref[0, :, cols(j)].astype(F32) * roles_ref[1, :, cols(j)].astype(F32)
        skips.append(jnp.sum(both, axis=0, keepdims=True))
        send_ref[j, :N] = local_sums(roles_ref, 0, j, w, low, p_t)
    skip = heads_of(jnp.concatenate(skips, axis=0))
    sub = iota((EXT, 128), 0)
    for j in range(PAIRS):
        send_ref[j, N:] = jnp.where(sub == 0, gain_ref[j : j + 1], jnp.where(sub == 1, skip, 0.0))


def own_kernel(
    _, len_ref, skip_gain_ref, roles_ref, rows_ref, w_ref, gain_ref, mine_ref, keep_ref, gains_ref
):
    low = iota((T, 128), 1) < 64
    p_t = rows_ref[1].T
    w = w_ref[1]
    for j in range(PAIRS):
        mine_ref[j, N:] = jnp.broadcast_to(gain_ref[j : j + 1], (EXT, 128))
        mine_ref[j, :N] = local_sums(roles_ref, 1, j, w, low, p_t)
        gains_ref[j : j + 1] = jnp.where(
            low[:1], skip_gain_ref[2 * j], skip_gain_ref[2 * j + 1]
        )
    base = block_base()
    starts = doc_starts(len_ref)
    offset = iota((EXT, T), 1)
    keep = jnp.ones((EXT, T), F32)
    for s in starts:
        keep = jnp.where(offset + base == s, 0.0, keep)
    keep_ref[...] = keep


def combine_kernel(recv_ref, mine_ref, send_ref, out_ref):
    sub = iota((EXT, 128), 0)
    for j in range(PAIRS):
        theirs = recv_ref[j, N:]
        ours = send_ref[j, N:]
        out_ref[j, :N] = theirs[:1] * mine_ref[j, :N] + recv_ref[j, :N]
        out_ref[j, N:] = jnp.where(sub == 0, theirs * ours, theirs + ours)


def scan_kernel(in_ref, skip_ref, out_ref, buffer, sems):
    first = is_first()
    running = jnp.zeros((N, 128), F32)
    skip = jnp.zeros((EXT, 128), F32)
    copies = []
    for i in range(PAIRS):
        at = jnp.where(first, i, PAIRS - 1 - i)
        buffer[i] = running
        copies.append(pltpu.make_async_copy(buffer.at[i], out_ref.at[at], sems.at[i]))
        copies[-1].start()
        if i < PAIRS - 1:
            running = in_ref[at, N : N + 1] * running + in_ref[at, :N]
        skip = skip + in_ref[i, N:]
    skip_ref[...] = jnp.broadcast_to(skip[1:2], (EXT, 128))
    for copy in copies:
        copy.wait()


def halves(x):
    high = x.astype(BF16)
    return high, (x - high.astype(F32)).astype(BF16)


def picked_sums(x, pick):
    high, low = halves(x)
    return dot(high, pick) + dot(low, pick)


def inside_kernel(
    _, len_ref, v_hbm, g_hbm, rows_ref, ld_ref, w_ref, gains_ref,
    raw_ref, change_ref, base_hbm, wt_hbm, pick_hbm,
    roles_ref, base_ref, wt_ref, pick_ref, sems, in_sems,
):
    first = is_first()
    v_slot = jnp.where(first, 1, 0)
    g_slot = 1 - v_slot
    fetch = [
        pltpu.make_async_copy(v_hbm.at[0], roles_ref.at[v_slot], in_sems.at[0]),
        pltpu.make_async_copy(g_hbm.at[0], roles_ref.at[g_slot], in_sems.at[1]),
    ]
    for copy in fetch:
        copy.start()
    base = block_base()
    starts = doc_starts(len_ref)
    ld = ld_ref[0]
    tri = lower_triangle()
    cum_t = add_up(dot(tri, third, NT) for third in thirds(ld))
    cum_h = add_up(dot(third, tri, NT) for third in thirds(ld))
    t_at = iota((T, T), 0)
    s_at = iota((T, T), 1)
    same = segments(starts, base, t_at) == segments(starts, base, s_at)
    bias = jnp.where(jnp.logical_and(s_at <= t_at, same), 0.0, FAR)
    b = rows_ref[v_slot]
    c = rows_ref[g_slot]
    scores = dot(c, b, NT)
    low = iota((T, 128), 1) < 64
    zero = jnp.zeros((T, 128), BF16)
    grad_scores = jnp.zeros((T, T), F32)
    changes = jnp.zeros((T, 128), F32)
    head = iota((128, 128), 1) - (iota((128, 128), 0) >= 64).astype(jnp.int32)
    copies = []
    for copy in fetch:
        copy.wait()
    for j in range(PAIRS):
        v = roles_ref[v_slot, :, cols(j)]
        g = roles_ref[g_slot, :, cols(j)]
        v_two = jnp.concatenate([jnp.where(low, v, zero), jnp.where(low, zero, v)], axis=0)
        g_two = jnp.concatenate([jnp.where(low, g, zero), jnp.where(low, zero, g)], axis=0)
        grad_mix = dot(g, v_two, NT)
        mixes = []
        for k in range(2):
            h = 2 * j + k
            decay = jnp.exp(cum_t[:, h : h + 1] - cum_h[h : h + 1, :] + bias)
            mixes.append((scores * decay).astype(BF16))
            grad_scores = grad_scores + grad_mix[:, k * T : (k + 1) * T] * decay
        within = dot(jnp.concatenate(mixes, axis=1), v_two)
        back = dot(jnp.concatenate(mixes, axis=0), g_two, TN)
        v = v.astype(F32)
        g = g.astype(F32)
        skip_row = gains_ref[j : j + 1]
        base_ref[g_slot, :, cols(j)] = within + skip_row * v
        base_ref[v_slot, :, cols(j)] = back + skip_row * g
        pick = (head == 2 * j).astype(BF16)
        pick_ref[cols(j)] = pick
        changes = changes + picked_sums(g * within - v * back, pick)
        for slot in range(2):
            wide = spread(w_ref[slot], j, low)
            own = roles_ref[slot, :, cols(j)].astype(F32)
            wt_ref[slot, :, cols(j)] = (own * wide).astype(BF16)
        if (j + 1) % (PAIRS // PARTS) == 0:
            k = j // (PAIRS // PARTS)
            part = slice(k * PART, (k + 1) * PART)
            for n, (src, dst) in enumerate(((base_ref, base_hbm), (wt_ref, wt_hbm))):
                copies.append(
                    pltpu.make_async_copy(
                        src.at[:, :, part], dst.at[:, :, part], sems.at[n, k]
                    )
                )
            copies.append(pltpu.make_async_copy(pick_ref.at[part], pick_hbm.at[part], sems.at[2, k]))
            for copy in copies[-3:]:
                copy.start()
    change_ref[...] = changes
    half = grad_scores.astype(BF16)
    raw_ref[g_slot] = dot(half, b)
    raw_ref[v_slot] = dot(half, c, TN)
    for copy in copies:
        copy.wait()


def pass_on_kernel(_, x_ref, mine_ref, s0_ref, s1_ref, s2_ref, s3_ref, out_ref, gain_ref):
    for j in range(PAIRS):
        gain = mine_ref[j, N : N + 1]
        gain_ref[j : j + 1] = gain
        out_ref[j * N : (j + 1) * N] = gain * x_ref[j] + mine_ref[j, :N]
    sub = iota((EXT, 128), 0)
    plane = lax.axis_index("dp") + 4 * lax.axis_index(CORE)
    ext = jnp.zeros((EXT, 128), F32)
    for k, ref in enumerate((s0_ref, s1_ref, s2_ref, s3_ref)):
        ext = jnp.where(sub == ((plane + k) & 7), ref[...], ext)
    out_ref[PAIRS * N :] = ext


def finish_role(x_of, rows, base_ref, w, wt_ref, work, before, emit):
    half_ref, hi_ref, lo_ref = work
    low = iota((T, 128), 1) < 64
    for j in range(PAIRS):
        before(j)
        half = x_of(j).astype(BF16)
        half_ref[:, cols(j)] = half
        read = dot(rows, half)
        tail = spread(w, j, low) * read
        change = wt_ref[:, cols(j)].astype(F32) * read
        hi_ref[:, cols(j)], lo_ref[:, cols(j)] = halves(change)
        emit(
            j,
            (base_ref[:, cols(j)] + tail).astype(BF16),
            jnp.sum(change, axis=0, keepdims=True),
        )


def near_kernel(
    _, x_ref, rows_ref, w_ref, raw_ref, base_hbm, wt_hbm, pick_hbm,
    out_ref, total_ref, change_ref, end_ref, pick_ref, base_far, wt_far,
    base_ref, wt_ref, half_ref, hi_ref, lo_ref, sems, far_sems,
):
    parts = []
    for k in range(PARTS):
        part = slice(k * PART, (k + 1) * PART)
        parts.append(
            (
                pltpu.make_async_copy(
                    base_hbm.at[0, :, part], base_ref.at[:, part], sems.at[0, k]
                ),
                pltpu.make_async_copy(
                    wt_hbm.at[0, :, part], wt_ref.at[:, part], sems.at[1, k]
                ),
            )
        )
        for copy in parts[-1]:
            copy.start()
    later = [
        pltpu.make_async_copy(pick_hbm, pick_ref, far_sems.at[0]),
        pltpu.make_async_copy(base_hbm.at[1], base_far, far_sems.at[1]),
        pltpu.make_async_copy(wt_hbm.at[1], wt_far, far_sems.at[2]),
    ]
    for copy in later:
        copy.start()

    def before(j):
        if j % (PAIRS // PARTS) == 0:
            for copy in parts[j // (PAIRS // PARTS)]:
                copy.wait()

    def emit(j, result, end):
        out_ref[:, cols(j)] = result
        end_ref[j : j + 1] = end

    work = (half_ref, hi_ref, lo_ref)
    finish_role(
        lambda j: x_ref[j], rows_ref[0], base_ref, w_ref[0], wt_ref, work, before, emit
    )
    later[0].wait()
    total_ref[...] = raw_ref[0] + dot(wt_ref[...], half_ref[...], NT)
    pick = pick_ref[...]
    change_ref[...] = dot(hi_ref[...], pick) + dot(lo_ref[...], pick)
    for copy in later[1:]:
        copy.wait()


def far_kernel(
    scales, y_ref, x_ref, passed_ref, rows_ref, w_ref, raw_ref, base_change_ref, gain_ref,
    keep_ref, near_ref, near_total_ref, near_change_ref, near_end_ref, pick_ref, base_ref,
    wt_ref,
    skip_ref, igrad_hbm, ograd_hbm, dgrad_hbm, mixed_hbm, vgrad_hbm,
    mixed_ref, vgrad_ref, igrad_ref, ograd_ref, dgrad_ref, sems, small_sems,
    half_ref, hi_ref, lo_ref,
):
    in_scale, out_scale, decay_scale, skip_scale = scales
    first = is_first()
    copies = []
    ends = []

    def emit(j, result, end):
        near = near_ref[:, cols(j)]
        mixed_ref[:, cols(j)] = jnp.where(first, near, result)
        vgrad_ref[:, cols(j)] = jnp.where(first, result, near)
        meet = jnp.sum(x_ref[j] * y_ref[j * N : (j + 1) * N], axis=0, keepdims=True)
        end = jnp.where(first, end, near_end_ref[j : j + 1])
        ends.append(end + gain_ref[j : j + 1] * meet)
        if (j + 1) % (PAIRS // PARTS) == 0:
            k = j // (PAIRS // PARTS)
            part = slice(k * PART, (k + 1) * PART)
            for n, (src, dst) in enumerate(((mixed_ref, mixed_hbm), (vgrad_ref, vgrad_hbm))):
                copies.append(
                    pltpu.make_async_copy(src.at[:, part], dst.at[0, :, part], sems.at[n, k])
                )
                copies[-1].start()

    work = (half_ref, hi_ref, lo_ref)
    finish_role(
        lambda j: y_ref[j * N : (j + 1) * N], rows_ref[1], base_ref, w_ref[1], wt_ref, work,
        lambda j: None, emit,
    )
    total = raw_ref[1] + dot(wt_ref[...], half_ref[...], NT)
    near_total = near_total_ref[...]
    igrad_ref[...] = jnp.where(first, total, near_total) * in_scale
    ograd_ref[...] = jnp.where(first, near_total, total) * out_scale
    small = [
        pltpu.make_async_copy(igrad_ref, igrad_hbm.at[0], small_sems.at[0]),
        pltpu.make_async_copy(ograd_ref, ograd_hbm.at[0], small_sems.at[1]),
        pltpu.make_async_copy(dgrad_ref, dgrad_hbm.at[0], small_sems.at[2]),
    ]
    small[0].start()
    small[1].start()
    pick = pick_ref[...]
    changes = near_change_ref[...] - (dot(hi_ref[...], pick) + dot(lo_ref[...], pick))
    changes = base_change_ref[...] + jnp.where(first, changes, -changes)
    at_end = iota((T, 128), 0) == T - 1
    changes = changes + jnp.where(at_end, heads_of(jnp.concatenate(ends, axis=0)), 0.0)
    tri = lower_triangle()
    summed = add_up(dot(third, tri, TN) for third in thirds(changes))[:HEADS]
    dgrad_ref[...] = summed * keep_ref[:1] * decay_scale
    small[2].start()
    skips = passed_ref[PAIRS * N :] + y_ref[PAIRS * N :]
    skip_ref[...] = jnp.sum(skips, axis=0, keepdims=True)[:, :HEADS] * skip_scale
    for copy in copies + small:
        copy.wait()


def call(kernel, outs, *args, after=(), spaces=(), out_spaces=(), scratch=(), flops=0, moved=0):
    in_specs = [ANY] * len(after) + list(spaces)
    in_specs += [VMEM] * (len(args) + len(after) - len(in_specs))
    out_specs = [VMEM] * (len(outs) - len(out_spaces)) + list(out_spaces)
    return pl.pallas_call(
        kernel,
        out_shape=tuple(outs),
        in_specs=in_specs,
        out_specs=tuple(out_specs),
        scratch_shapes=list(scratch),
        compiler_params=pltpu.CompilerParams(vmem_limit_bytes=20 << 20),
        cost_estimate=pl.CostEstimate(flops=flops, bytes_accessed=moved, transcendentals=0),
    )(*after, *args)


def f32(*shape):
    return jax.ShapeDtypeStruct(shape, F32)


def bf16(*shape):
    return jax.ShapeDtypeStruct(shape, BF16)


def dma(*shape):
    return pltpu.SemaphoreType.DMA(shape)


def swap_cores(x):
    return lax.ppermute(x, CORE, [(0, 1), (1, 0)])


def exchange(x):
    return lax.all_to_all(x, CHIPS, split_axis=0, concat_axis=0, tiled=True)


def from_plane(x, offset):
    pairs = []
    for d in range(8):
        for c in range(2):
            pairs.append((((d + 4 * c + offset) % 8) * 2 + c, d * 2 + c))
    return lax.ppermute(x, ("dp", CORE), pairs)


def body(values_in, input_proj, output_proj, log_decay, doc_lengths, skip_gain, out_cotangent):
    inputs = (doc_lengths, values_in, out_cotangent, input_proj, output_proj, log_decay)
    token_count = lax.axis_size(SEQ) * T
    seq_count = lax.axis_size("dp")
    inner = values_in.shape[2]
    head_dim = inner // HEADS
    loaded = f32(PAIRS, N + EXT, 128)
    plain = f32(PAIRS, N, 128)
    roles, rows, w, gain, send = call(
        prep_kernel,
        (bf16(2, T, inner), bf16(2, T, N), f32(2, T, HEADS), f32(PAIRS, 128), loaded),
        *(pltpu.with_memory_space_constraint(a, pltpu.HBM) for a in inputs),
        spaces=[HBM] * 6,
        scratch=[
            pltpu.SMEM((1, DOCS), jnp.int32), pltpu.VMEM((HEADS, T), F32),
            dma(4), dma(PARTS), dma(PARTS),
        ],
        moved=4 << 20,
    )
    recv = swap_cores(send)
    mine, keep, gains = call(
        own_kernel,
        (loaded, f32(EXT, T), f32(PAIRS, 128)),
        doc_lengths, skip_gain, roles, rows, w, gain,
        after=(send,),
        spaces=[SMEM] * 2,
        moved=4 << 20,
    )
    (chip,) = call(combine_kernel, (loaded,), recv, mine, send, moved=3 << 20)
    gathered = exchange(chip)
    skip, prefix = call(
        scan_kernel,
        (f32(EXT, 128), pltpu.HBM((PAIRS, N, 128), F32)),
        gathered,
        out_spaces=[HBM],
        scratch=[pltpu.VMEM((PAIRS, N, 128), F32), dma(PAIRS)],
        moved=2 << 20,
    )
    x = exchange(prefix)
    wide16 = pltpu.VMEM((T, inner), BF16)
    wide32 = pltpu.VMEM((T, inner), F32)
    skips = [from_plane(skip, k) for k in range(4)]
    raw, change, *factors = call(
        inside_kernel,
        (
            f32(2, T, N), f32(T, 128), pltpu.HBM((2, T, inner), F32),
            pltpu.HBM((2, T, inner), BF16), pltpu.HBM((inner, 128), BF16),
        ),
        doc_lengths,
        *(pltpu.with_memory_space_constraint(a, pltpu.HBM) for a in (values_in, out_cotangent)),
        rows, log_decay, w, gains,
        after=(skip,),
        spaces=[SMEM, HBM, HBM],
        out_spaces=[HBM] * 3,
        scratch=[
            pltpu.VMEM((2, T, inner), BF16), pltpu.VMEM((2, T, inner), F32),
            pltpu.VMEM((2, T, inner), BF16), pltpu.VMEM((inner, 128), BF16),
            dma(3, PARTS), dma(2),
        ],
        moved=12 << 20,
    )
    passed, gain = call(
        pass_on_kernel,
        (f32(PAIRS * N + EXT, 128), f32(PAIRS, 128)),
        x, mine, *skips,
        after=(raw,),
        moved=3 << 20,
    )
    y = swap_cores(passed)
    near = call(
        near_kernel,
        (
            bf16(T, inner), f32(T, N), f32(T, 128), f32(PAIRS, 128), bf16(inner, 128),
            f32(T, inner), bf16(T, inner),
        ),
        x, rows, w, raw,
        *(pltpu.with_memory_space_constraint(a, pltpu.HBM) for a in factors),
        after=(passed,),
        spaces=[VMEM] * 4 + [HBM] * 3,
        scratch=[wide32, wide16, wide16, wide16, wide16, dma(2, PARTS), dma(3)],
        moved=8 << 20,
    )
    scales = (
        1.0 / inner**0.5,
        (N / (inner * token_count)) ** 0.5,
        1.0 / (head_dim * token_count) ** 0.5,
        1.0 / (seq_count * token_count * head_dim) ** 0.5,
    )
    skip_grad, input_grad, output_grad, decay_grad, mixed, values_grad = call(
        functools.partial(far_kernel, scales),
        (
            f32(1, HEADS), f32(1, T, N), f32(1, T, N), f32(1, HEADS, T),
            bf16(1, T, inner), bf16(1, T, inner),
        ),
        y, x, passed, rows, w, raw, change, gain, keep, *near,
        out_spaces=[HBM] * 5,
        scratch=[
            wide16, wide16, pltpu.VMEM((T, N), F32), pltpu.VMEM((T, N), F32),
            pltpu.VMEM((HEADS, T), F32), dma(2, PARTS), dma(3), wide16, wide16, wide16,
        ],
        moved=8 << 20,
    )
    return mixed, values_grad, input_grad, output_grad, decay_grad, skip_grad[0]


def solution(mesh):
    finer = Mesh(mesh.devices.reshape(mesh.shape["dp"], 4, 4, 2), ("dp",) + SEQ)
    placed = (
        P("dp", SEQ, None),
        P("dp", SEQ, None),
        P("dp", SEQ, None),
        P("dp", None, SEQ),
        P("dp", None),
        P(),
        P("dp", SEQ, None),
    )
    return jax.shard_map(
        body,
        mesh=finer,
        in_specs=placed,
        out_specs=(
            P("dp", SEQ, None),
            P("dp", SEQ, None),
            P("dp", SEQ, None),
            P("dp", SEQ, None),
            P("dp", None, SEQ),
            P(),
        ),
        check_vma=False,
    )
```
